512 devices in a mesh: dp: 128 (over z, y, core), tensor: 4 (over x).
Axes of the slice: x: 4, y: 8, z: 8, core: 2. Of those that a mesh axis runs over, the one named last changes fastest.
Arguments:
- hidden: bfloat16 [65536, 1024], P('dp', 'tensor'), may hold values from -24 to 24
- gain: float32 [1024], replicated, may hold values from 0.5 to 1.5
- head_weight: bfloat16 [1024, 25600], P(None, ('tensor', 'dp')), may hold values from -6 to 6
- targets: int32 [65536], P('dp'), may hold values from 0 to 25599
- row_count: int32 [128], P('dp'), may hold values from 64 to 512, as said below
- dest: int32 [65536], P('dp'), may hold values from 0 to 65535, as said below
Outputs:
- logprob: float32 [65536], P('dp')
- entropy: float32 [65536], P('dp')
The draws below stay inside these ranges and needn't reach their ends.
Inputs may be any that keep to these rules, and one draw needn't show every extreme that they name: Each device's live slots are its first row_count ones; at least one device is full. dest is a permutation. Slot results of device s go to device dest // 512; every device sends exactly 4 results to every device, those from device s fill positions s * 4 to (s + 1) * 4 - 1 of the receiver's block, in the order of their position in the sender's slots sorted by destination.
All inputs are finite; a program needn't handle non-finite values.
Results may differ from the reference program's by a relative error of at most 0.0062.
Values may be sent and summed in bfloat16 or wider, within the bound.
A program may use at most 128 MiB of HBM per device.

```python
import math
import jax
import jax.numpy as jnp
import numpy as np
from jax import lax

D = 1024
VOCAB = 25600
TOK_DEV = 512
TOKENS = 65536
GROUPS = 128
RETURN_ROWS = 4


spike_count = 64


def head_matrix(key):
    base = jnp.clip(jax.random.normal(jax.random.fold_in(key, 3), (D, VOCAB), jnp.float32), -5.0, 5.0) * (3.0 / math.sqrt(D))
    columns = jax.random.permutation(jax.random.fold_in(key, 4), VOCAB)[:spike_count]
    level = jax.random.uniform(jax.random.fold_in(key, 5), (spike_count,), jnp.float32, 120.0, 360.0)
    spacing = jax.random.uniform(jax.random.fold_in(key, 6), (spike_count,), jnp.float32, 1.0, 3.0)
    signs = jax.random.randint(jax.random.fold_in(key, 10), (D, spike_count), 0, 2).astype(jnp.float32) * 2.0 - 1.0
    chosen = signs * (level / D)[None, :]
    second = chosen * (1.0 - spacing / level)[None, :]
    base = base.at[:, columns].set(chosen)
    base = base.at[:, (columns + VOCAB // 2 + 7) % VOCAB].set(second)
    return (base, signs)


def draw_head_weight(key, part):
    base, signs = head_matrix(key)
    return base.astype(jnp.bfloat16)


def draw_hidden(key, part):
    states = jnp.clip(jax.random.normal(jax.random.fold_in(key, 7), (TOKENS, D), jnp.float32), -6.0, 6.0)
    base, signs = head_matrix(key)
    picked_rows = jax.random.randint(jax.random.fold_in(key, 8), (spike_count,), 0, TOKENS)
    states = states.at[picked_rows].set(signs.T * 4.0)
    return jnp.clip(states, -24.0, 24.0).astype(jnp.bfloat16)


def draw_row_count(key, part):
    counts = jax.random.randint(jax.random.fold_in(key, 1), (GROUPS,), TOK_DEV // 8, TOK_DEV + 1)
    fullest = jax.random.randint(jax.random.fold_in(key, 2), (), 0, GROUPS)
    return counts.at[fullest].set(TOK_DEV).astype(jnp.int32)


def draw_dest(key, part):
    keys = jax.random.split(jax.random.fold_in(key, 11), GROUPS)
    orders = jax.vmap(lambda single: jax.random.permutation(single, TOK_DEV))(keys)
    source = jnp.arange(GROUPS, dtype=jnp.int32)[:, None]
    owner = orders % GROUPS
    within = source * RETURN_ROWS + orders // GROUPS
    return (owner * TOK_DEV + within).reshape(TOKENS).astype(jnp.int32)


def place_ends(result, rng, smallest, high):
    spot = [jax.random.randint(jax.random.fold_in(rng, axis), (), 0, length) for axis, length in enumerate(result.shape)]
    widest = result.shape.index(max(result.shape))
    next_to = spot[:widest] + [(spot[widest] + 1) % result.shape[widest]] + spot[widest + 1:]
    return result.at[tuple(spot)].set(smallest).at[tuple(next_to)].set(high)


def rank_bounds(amount, skew):
    loads = [(1 << 20) // math.isqrt(standing ** skew) + 1 for standing in range(1, amount + 1)]
    spread = 1 + sum(loads) // (1 << 30)
    return np.cumsum(np.array([max(1, weight // spread) for weight in loads]))


def skewed_ids(own_key, shape, count, skew):
    listing = rank_bounds(count, skew)
    lot = jax.random.randint(jax.random.fold_in(own_key, 1), shape, 0, int(listing[count - 1]))
    grade = jnp.searchsorted(jnp.asarray(listing, jnp.int32), lot, side="right")
    return jax.random.permutation(jax.random.fold_in(own_key, 2), count)[grade].astype(jnp.int32)


def setup_inputs(seed: int = 0) -> dict:
    streams_of = jax.random.split(jax.random.key(seed), 7)
    return {
        "hidden": draw_hidden(jax.random.fold_in(streams_of[6], 71), 0),
        "gain": jnp.clip(1.0 + 0.1 * jax.random.normal(streams_of[1], (D,), jnp.float32), 0.5, 1.5),
        "head_weight": draw_head_weight(jax.random.fold_in(streams_of[6], 71), 0),
        "targets": place_ends(skewed_ids(streams_of[3], (TOKENS,), VOCAB, 2), jax.random.fold_in(streams_of[3], 3), 0, VOCAB - 1).astype(jnp.int32),
        "row_count": draw_row_count(jax.random.fold_in(streams_of[6], 71), 0),
        "dest": draw_dest(jax.random.fold_in(streams_of[6], 71), 0),
    }


def reference(hidden, gain, head_weight, targets, row_count, dest):
    groups = TOKENS // TOK_DEV
    blocks = hidden.reshape(groups, TOK_DEV, D)
    wanted = targets.reshape(groups, TOK_DEV)

    def one_group(args):
        states, tokens, count = args
        wide = states.astype(jnp.float32)
        power = lax.optimization_barrier(jnp.mean(wide * wide, axis=1, keepdims=True))
        normed = (wide * lax.rsqrt(power + 1e-06) * gain.astype(jnp.float32)).astype(jnp.bfloat16)
        logits = jnp.dot(normed, head_weight, preferred_element_type=jnp.float32)
        top = lax.optimization_barrier(jnp.max(logits, axis=1, keepdims=True))
        weights = jnp.exp(logits - top)
        mass = lax.optimization_barrier(jnp.sum(weights, axis=1))
        moment = lax.optimization_barrier(jnp.sum(weights * logits, axis=1))
        lse = top[:, 0] + jnp.log(mass)
        picked = jnp.take_along_axis(logits, tokens[:, None].astype(jnp.int32), axis=1)[:, 0]
        live = jnp.arange(TOK_DEV, dtype=jnp.int32) < count
        value_lp = jnp.where(live, picked - lse, 0.0)
        value_ent = jnp.where(live, lse - moment / mass, 0.0)
        return (value_lp, value_ent)
    value_lp, value_ent = lax.map(one_group, (blocks, wanted, row_count))
    logprob = jnp.zeros((TOKENS,), jnp.float32).at[dest].set(value_lp.reshape(TOKENS))
    entropy = jnp.zeros((TOKENS,), jnp.float32).at[dest].set(value_ent.reshape(TOKENS))
    return (logprob, entropy)
```

```python
import jax
import jax.numpy as jnp
from jax import lax
from jax.sharding import Mesh, PartitionSpec as P


def stats_of(logits_t, wanted):
    top = jnp.max(logits_t, axis=0)
    weights = jnp.exp(logits_t - top[None, :])
    mass = jnp.sum(weights, axis=0)
    moment = jnp.sum(weights * logits_t, axis=0)
    ids = lax.broadcasted_iota(jnp.int32, logits_t.shape, 0)
    picked = jnp.sum(jnp.where(ids == wanted[None, :], logits_t, 0.0), axis=0)
    return jnp.stack([top, mass, moment, picked])


def merge(parts):
    top = jnp.max(parts[:, 0], axis=0)
    factor = jnp.exp(parts[:, 0] - top[None])
    mass = jnp.sum(parts[:, 1] * factor, axis=0)
    moment = jnp.sum(parts[:, 2] * factor, axis=0)
    return top, mass, moment, jnp.sum(parts[:, 3], axis=0)


def body(hidden, gain, head_weight, targets, row_count, dest):
    rows = hidden.shape[0]
    cols = head_weight.shape[1]
    padded = -(-cols // 8) * 8
    groups = lax.axis_size("zy") * 2
    tensors = lax.axis_size("tensor")
    core = lax.axis_index("core")
    mine = lax.axis_index("tensor")
    swap = [(0, 1), (1, 0)]
    spread = jnp.pad(head_weight.T, ((0, padded - cols), (0, 0)))
    piece = lax.all_gather(spread, "zy", axis=0, tiled=True)
    shards = [hidden]
    for step in range(1, tensors):
        shards.append(lax.ppermute(hidden, "tensor", [((i + step) % tensors, i) for i in range(tensors)]))
    own = jnp.stack(shards)
    other = lax.ppermute(own, "core", swap)
    both = jnp.concatenate([own, other], axis=1).astype(jnp.float32)
    power = jnp.sum(both * both, axis=(0, 2)) / (tensors * hidden.shape[1])
    scale = lax.rsqrt(power + 1e-06)
    gains = jnp.roll(gain.reshape(tensors, -1), -mine, axis=0)
    turned = (both * scale[None, :, None] * gains[:, None, :]).astype(jnp.bfloat16)
    ordered = jnp.roll(turned, mine, axis=0)
    normed = jnp.moveaxis(ordered, 0, 1).reshape(2 * rows, -1)
    wanted = jnp.concatenate([targets, lax.ppermute(targets, "core", swap)])
    local = wanted - mine * (cols * groups)
    device = local // cols
    ok = (local >= 0) & (device < groups) & (device % 2 == core)
    slot = jnp.where(ok, (device // 2) * padded + local % cols, -1)
    logits = lax.dot_general(piece, normed, (((1,), (1,)), ((), ())), preferred_element_type=jnp.float32)
    ids = lax.broadcasted_iota(jnp.int32, logits.shape, 0)
    logits = jnp.where(ids % padded < cols, logits, -1e30)
    stats = stats_of(logits, slot)
    theirs = lax.ppermute(stats[:, rows:], "core", swap)
    pair = jnp.stack(merge(jnp.stack([stats[:, :rows], theirs])))
    top, mass, moment, picked = merge(lax.all_gather(pair, "tensor", axis=0))
    live = jnp.arange(rows, dtype=jnp.int32) < row_count[0]
    lse = top + jnp.log(mass)
    value_lp = jnp.where(live, picked - lse, 0.0)
    value_ent = jnp.where(live, lse - moment / mass, 0.0)
    share = rows // groups
    rank = (dest // rows) * share + dest % share
    hit = lax.broadcasted_iota(jnp.int32, (rows, rows), 0) == rank[None, :]
    sent = [jnp.sum(jnp.where(hit, v[None, :], 0.0), axis=1).reshape(groups, share) for v in (value_lp, value_ent)]
    got = lax.all_to_all(jnp.concatenate(sent, axis=1), ("zy", "core"), 0, 0, tiled=True)
    return got[:, :share].reshape(rows), got[:, share:].reshape(rows)


def solution(mesh):
    dp, tensor = mesh.devices.shape
    fine = Mesh(mesh.devices.reshape(dp // 2, 2, tensor), ("zy", "core", "tensor"))
    group = ("zy", "core")
    in_specs = (P(group, "tensor"), P(), P(None, ("tensor", "zy", "core")), P(group), P(group), P(group))
    return jax.shard_map(body, mesh=fine, in_specs=in_specs, out_specs=(P(group), P(group)), check_vma=False)
```

```python
import functools

import jax
import jax.numpy as jnp
from jax import lax
from jax.experimental import pallas as pl
from jax.experimental.pallas import tpu as pltpu
from jax.sharding import Mesh, PartitionSpec as P

RING = 8
TENSORS = 4
MAIN = 48
CHUNK = 256
F32 = jnp.float32


def zigzag(i):
    return ((i + 1) >> 1) * (1 - 2 * (i & 1))


def head_kernel(main_hbm, rest_hbm, hid_hbm, code_hbm, gain_ref, out_ref,
                wbuf, lbuf, hbuf, cbuf, normed, wide_rest, rest, stats, packed, gath,
                w_recv, w_send, h_recv, h_send, c_sem, s_recv, s_send, local_sem):
    z, y = lax.axis_index("z"), lax.axis_index("y")
    core, x = lax.axis_index("core"), lax.axis_index("tensor")
    rows = hid_hbm.shape[1]
    feats = hid_hbm.shape[0]
    p = z + core * (y - z)
    q = y + core * (z - y)

    def wrap(v):
        return (v + 2 * RING) & (RING - 1)

    def at(pp, qq):
        return (pp + core * (qq - pp), qq + core * (pp - qq), core, x)

    def at_x(xx, cc):
        return (z, y, cc, (xx + 2 * TENSORS) & (TENSORS - 1))

    right1, left1 = at(wrap(p + 1), q), at(wrap(p - 1), q)
    right2, left2 = at(p, wrap(q + 1)), at(p, wrap(q - 1))
    partner = at_x(x, 1 - core)
    slot0 = q * RING + p

    locals_ = [
        pltpu.make_async_copy(main_hbm, wbuf.at[slot0], local_sem.at[0]),
        pltpu.make_async_copy(rest_hbm, lbuf.at[slot0], local_sem.at[1]),
        pltpu.make_async_copy(hid_hbm, hbuf.at[core, x], local_sem.at[2]),
        pltpu.make_async_copy(code_hbm, cbuf.at[core], local_sem.at[3]),
    ]
    for copy in locals_:
        copy.start()
    barrier = pltpu.get_barrier_semaphore()
    peers = [at_x(x + d, c) for d in range(TENSORS) for c in (core, 1 - core)][1:]
    for peer in [right1, left1, right2, left2] + peers:
        pl.semaphore_signal(barrier, inc=1, device_id=peer, device_id_type=pl.DeviceIdType.MESH)
    for copy in locals_:
        copy.wait()
    pl.semaphore_wait(barrier, 4 + len(peers))

    def block(slot, kind, target):
        return [
            pltpu.make_async_remote_copy(
                src_ref=buf.at[slot], dst_ref=buf.at[slot],
                send_sem=w_send.at[kind, n, slot], recv_sem=w_recv.at[n, slot],
                device_id=target, device_id_type=pl.DeviceIdType.MESH)
            for n, buf in enumerate((wbuf, lbuf))
        ]

    def start(slot, kind, target):
        for copy in block(slot, kind, target):
            copy.start()

    def arrive(slot):
        for copy in block(slot, 0, right1):
            copy.wait_recv()

    def sent(slot, kind):
        for copy in block(slot, kind, right1):
            copy.wait_send()

    def states(cc, xx, kind, target):
        xs = (xx + 2 * TENSORS) & (TENSORS - 1)
        return pltpu.make_async_remote_copy(
            src_ref=hbuf.at[cc, xs], dst_ref=hbuf.at[cc, xs],
            send_sem=h_send.at[kind, xs], recv_sem=h_recv.at[cc, xs],
            device_id=target, device_id_type=pl.DeviceIdType.MESH)

    codes = pltpu.make_async_remote_copy(
        src_ref=cbuf.at[core], dst_ref=cbuf.at[core], send_sem=c_sem.at[0], recv_sem=c_sem.at[1],
        device_id=partner, device_id_type=pl.DeviceIdType.MESH)
    way = 1 - 2 * core
    start(slot0, 0, right1)
    start(slot0, 1, left1)
    states(core, x, 0, at_x(x + 1, core)).start()
    states(core, x, 1, at_x(x - 1, core)).start()
    states(core, x, 3, partner).start()
    codes.start()
    start(slot0, 2, right2)
    start(slot0, 3, left2)

    def first(i):
        slot = q * RING + wrap(p + zigzag(i))
        arrive(slot)
        if i in (1, 3, 5):
            start(slot, 0, right1)
        if i in (2, 4):
            start(slot, 1, left1)
        start(slot, 2, right2)
        start(slot, 3, left2)

    for i in range(1, 4):
        first(i)
    for d in (-1, 1):
        states(core, x + d, 0, partner).wait_recv()
    states(core, x - way, 2, at_x(x + way, core)).start()
    for d in (-1, 1):
        states(core, x + d, 3, partner).start()
    for i in range(4, 8):
        first(i)

    def from_left(t, i, forward):
        slot = wrap(q - t) * RING + wrap(p + zigzag(i))
        arrive(slot)
        if forward:
            start(slot, 2, right2)

    def from_right(t, i, forward):
        slot = wrap(q + t) * RING + wrap(p + zigzag(i))
        arrive(slot)
        if forward:
            start(slot, 3, left2)

    def both(t, low, high):
        @pl.loop(low, high)
        def _(i):
            from_left(t, i, True)
            from_right(t, i, True)

    both(1, 0, 4)
    states(core, x + 2, 0, partner).wait_recv()
    states(core, x + 2, 3, partner).start()
    both(1, 4, 8)

    for d in range(TENSORS):
        states(1 - core, x + d, 0, partner).wait_recv()
    codes.wait_recv()
    for c in range(2):
        power = jnp.zeros((1, rows), F32)
        for d in range(TENSORS):
            part = hbuf[c, d].astype(F32)
            power += jnp.sum(part * part, axis=0, keepdims=True)
        scale = lax.rsqrt(power / (TENSORS * feats) + 1e-06)
        for d in range(TENSORS):
            span = pl.ds(d * feats, feats)
            part = hbuf[c, d].astype(F32) * scale * gain_ref[span, :]
            normed[span, pl.ds(c * rows, rows)] = part.astype(jnp.bfloat16)
    stats[0] = jnp.full(stats.shape[1:], -1e30, F32)
    for n in range(1, 4):
        stats[n] = jnp.zeros(stats.shape[1:], F32)
    mine = (x * 2 + core) * 4096
    per = rows // CHUNK

    def update(weights, count, base, r):
        cols = pl.ds(pl.multiple_of(r * CHUNK, CHUNK), CHUNK)
        logits = jnp.dot(weights, normed[:, cols], preferred_element_type=F32)
        cube = logits.reshape(count // 8, 8, CHUNK)
        half = r // per
        span = pl.ds(pl.multiple_of((r - half * per) * CHUNK, CHUNK), CHUNK)
        wanted = cbuf[half, :, span] - (mine + base)
        ids = lax.broadcasted_iota(jnp.int32, (count, CHUNK), 0)
        old = stats[0, :, cols]
        top = jnp.maximum(old, jnp.max(cube, axis=0))
        factor = jnp.exp(old - top)
        weight = jnp.exp(cube - top[None])
        stats[0, :, cols] = top
        stats[1, :, cols] = stats[1, :, cols] * factor + jnp.sum(weight, axis=0)
        stats[2, :, cols] = stats[2, :, cols] * factor + jnp.sum(weight * cube, axis=0)
        hit = jnp.where(ids == wanted, logits, 0.0).reshape(count // 8, 8, CHUNK)
        stats[3, :, cols] = stats[3, :, cols] + jnp.sum(hit, axis=0)

    chunks = 2 * per

    def unit(u):
        k = u // chunks
        r = u - k * chunks
        g = wrap(q + zigzag(k))
        weights = wbuf[pl.ds(pl.multiple_of(g * RING, RING), RING)].reshape(RING * MAIN, -1)
        update(weights, RING * MAIN, g * (RING * MAIN), r)

    @pl.loop(0, 8)
    def _(i):
        from_left(2, i, True)
        from_right(2, i, True)
        unit(i)

    @pl.loop(0, 4)
    def _(i):
        from_left(3, i, True)
        from_right(3, i, False)
        unit(8 + i)

    @pl.loop(4, 8)
    def _(i):
        from_left(3, i, False)
        from_right(3, i, True)
        unit(8 + i)

    @pl.loop(0, 4)
    def _(i):
        from_left(4, i, False)
        unit(16 + 2 * i)
        from_right(4, i + 4, False)
        unit(17 + 2 * i)

    @pl.loop(24, 32)
    def _(u):
        unit(u)

    total = RING * RING * 2
    wide_rest[...] = lbuf[...].astype(F32).reshape(total * 8, 128)
    for k in range(8):
        rest[:, pl.ds(k * 128, 128)] = wide_rest[pl.ds(k, total, stride=8), :].astype(jnp.bfloat16)

    @pl.loop(0, chunks)
    def _(r):
        update(rest[...], total, RING * RING * MAIN, r)

    top = jnp.max(stats[0], axis=0, keepdims=True)
    factor = jnp.exp(stats[0] - top)
    lines = [top] + [jnp.sum(stats[n] * factor, axis=0, keepdims=True) for n in (1, 2)]
    lines.append(jnp.sum(stats[3], axis=0, keepdims=True))
    for c in range(2):
        for n, line in enumerate(lines):
            packed[c, pl.ds(n, 1), :] = line[:, c * rows:(c + 1) * rows]
        packed[c, pl.ds(4, 4), :] = jnp.zeros((4, rows), F32)
    who = x * 2 + core

    def result(n, peer):
        return pltpu.make_async_remote_copy(
            src_ref=packed.at[peer[2]], dst_ref=gath.at[who],
            send_sem=s_send.at[n], recv_sem=s_recv.at[who],
            device_id=peer, device_id_type=pl.DeviceIdType.MESH)

    def result_from(n, peer):
        source = peer[3] * 2 + peer[2]
        return pltpu.make_async_remote_copy(
            src_ref=packed.at[core], dst_ref=gath.at[source],
            send_sem=s_send.at[n], recv_sem=s_recv.at[source],
            device_id=peer, device_id_type=pl.DeviceIdType.MESH)

    for n, peer in enumerate(peers):
        result(n, peer).start()
    own = pltpu.make_async_copy(packed.at[core], gath.at[who], local_sem.at[0])
    own.start()

    for t in range(4):
        sent(q * RING + wrap(p - t), 0)
    for t in range(3):
        sent(q * RING + wrap(p + t), 1)

    @pl.loop(0, 8)
    def _(i):
        pp = wrap(p + zigzag(i))
        for t in range(3):
            sent(wrap(q - t) * RING + pp, 2)
            sent(wrap(q + t) * RING + pp, 3)

    @pl.loop(0, 4)
    def _(i):
        sent(wrap(q - 3) * RING + wrap(p + zigzag(i)), 2)
        sent(wrap(q + 3) * RING + wrap(p + zigzag(i + 4)), 3)

    states(core, x, 0, partner).wait_send()
    states(core, x, 1, partner).wait_send()
    states(core, x - way, 2, partner).wait_send()
    for d in range(TENSORS):
        states(core, x + d, 3, partner).wait_send()
    codes.wait_send()
    own.wait()
    for n, peer in enumerate(peers):
        result_from(n, peer).wait_recv()
        result(n, peer).wait_send()
    out_ref[...] = gath[...]


def head(main, rest, hid, code, gain):
    rows, feats, slots = hid.shape[1], hid.shape[0], RING * RING
    depth = TENSORS * feats
    any_space = pl.BlockSpec(memory_space=pl.ANY)
    vmem = pl.BlockSpec(memory_space=pltpu.VMEM)
    dma = pltpu.SemaphoreType.DMA
    return pl.pallas_call(
        head_kernel,
        out_shape=jax.ShapeDtypeStruct((2 * TENSORS, 8, rows), F32),
        in_specs=[any_space] * 4 + [vmem],
        out_specs=vmem,
        scratch_shapes=[
            pltpu.VMEM((slots, MAIN, depth), jnp.bfloat16),
            pltpu.VMEM((slots, 16, 128), jnp.bfloat16),
            pltpu.VMEM((2, TENSORS, feats, rows), jnp.bfloat16),
            pltpu.VMEM((2, 1, rows), jnp.int32),
            pltpu.VMEM((depth, 2 * rows), jnp.bfloat16),
            pltpu.VMEM((slots * 16, 128), F32),
            pltpu.VMEM((slots * 2, depth), jnp.bfloat16),
            pltpu.VMEM((4, 8, 2 * rows), F32),
            pltpu.VMEM((2, 8, rows), F32),
            pltpu.VMEM((2 * TENSORS, 8, rows), F32),
            dma((2, slots)), dma((4, 2, slots)), dma((2, TENSORS)), dma((4, TENSORS)),
            dma((2,)), dma((2 * TENSORS,)), dma((2 * TENSORS,)), dma((4,)),
        ],
        compiler_params=pltpu.CompilerParams(
            collective_id=0, has_side_effects=True, vmem_limit_bytes=48 << 20),
    )(main, rest, hid, code, gain)


def body(hidden, gain, head_weight, targets, row_count, dest):
    rows = hidden.shape[0]
    cols = head_weight.shape[1]
    groups = 2 * RING * RING
    turned = head_weight.T
    rest = turned[MAIN:].reshape(16, 128)
    owner, column = targets // (cols * groups), targets % cols
    device = (targets // cols) % groups
    near, zy = device % 2, device // 2
    zi, yi = zy // RING, zy % RING
    slot = jnp.where(near == 0, yi * RING + zi, zi * RING + yi)
    index = jnp.where(column < MAIN, slot * MAIN + column, RING * RING * MAIN + slot * 2 + column - MAIN)
    code = ((owner * 2 + near) * 4096 + index).reshape(1, rows)
    parts = head(turned[:MAIN], rest, hidden.T, code, gain.reshape(-1, 1))
    top = jnp.max(parts[:, 0], axis=0)
    factor = jnp.exp(parts[:, 0] - top[None])
    mass = jnp.sum(parts[:, 1] * factor, axis=0)
    moment = jnp.sum(parts[:, 2] * factor, axis=0)
    picked = jnp.sum(parts[:, 3], axis=0)
    live = jnp.arange(rows, dtype=jnp.int32) < row_count[0]
    lse = top + jnp.log(mass)
    value_lp = jnp.where(live, picked - lse, 0.0)
    value_ent = jnp.where(live, lse - moment / mass, 0.0)
    share = rows // groups
    rank = (dest // rows) * share + dest % share
    hit = lax.broadcasted_iota(jnp.int32, (rows, rows), 0) == rank[None, :]
    sent = [jnp.sum(jnp.where(hit, v[None, :], 0.0), axis=1).reshape(groups, share) for v in (value_lp, value_ent)]
    got = lax.all_to_all(jnp.concatenate(sent, axis=1), ("z", "y", "core"), 0, 0, tiled=True)
    return got[:, :share].reshape(rows), got[:, share:].reshape(rows)


def solution(mesh):
    tensor = mesh.devices.shape[1]
    fine = Mesh(mesh.devices.reshape(RING, RING, 2, tensor), ("z", "y", "core", "tensor"))
    group = ("z", "y", "core")
    in_specs = (P(group, "tensor"), P(), P(None, ("tensor", "z", "y", "core")), P(group), P(group), P(group))
    return jax.shard_map(body, mesh=fine, in_specs=in_specs, out_specs=(P(group), P(group)), check_vma=False)
```

```python
import functools

import jax
import jax.numpy as jnp
from jax import lax
from jax.experimental import pallas as pl
from jax.experimental.pallas import tpu as pltpu
from jax.sharding import Mesh, PartitionSpec as P

RING = 8
TENSORS = 4
MAIN = 48
CHUNK = 256
F32 = jnp.float32


def zigzag(i):
    return ((i + 1) >> 1) * (1 - 2 * (i & 1))


def head_kernel(main_hbm, rest_hbm, hid_hbm, code_hbm, gain_ref, place_ref, live_ref, out_ref,
                wbuf, lbuf, hbuf, cbuf, normed, wide_rest, rest, stats, packed, gath,
                select, values, line_out, line_in, plane_out, plane_in,
                w_recv, w_send, h_recv, h_send, c_sem, s_recv, s_send, local_sem,
                l_recv, l_send, p_recv, p_send):
    z, y = lax.axis_index("z"), lax.axis_index("y")
    core, x = lax.axis_index("core"), lax.axis_index("tensor")
    rows = hid_hbm.shape[1]
    feats = hid_hbm.shape[0]
    p = z + core * (y - z)
    q = y + core * (z - y)

    def wrap(v):
        return (v + 2 * RING) & (RING - 1)

    def at(pp, qq):
        return (pp + core * (qq - pp), qq + core * (pp - qq), core, x)

    def at_x(xx, cc):
        return (z, y, cc, (xx + 2 * TENSORS) & (TENSORS - 1))

    right1, left1 = at(wrap(p + 1), q), at(wrap(p - 1), q)
    right2, left2 = at(p, wrap(q + 1)), at(p, wrap(q - 1))
    partner = at_x(x, 1 - core)
    slot0 = q * RING + p

    locals_ = [
        pltpu.make_async_copy(main_hbm.at[pl.ds(0, MAIN)], wbuf.at[slot0], local_sem.at[0]),
        pltpu.make_async_copy(rest_hbm, lbuf.at[slot0], local_sem.at[1]),
        pltpu.make_async_copy(hid_hbm, hbuf.at[core, x], local_sem.at[2]),
        pltpu.make_async_copy(code_hbm, cbuf.at[core], local_sem.at[3]),
    ]
    for copy in locals_:
        copy.start()
    barrier = pltpu.get_barrier_semaphore()
    peers = [at_x(x + d, c) for d in range(TENSORS) for c in (core, 1 - core)][1:]
    for peer in [right1, left1, right2, left2] + peers:
        pl.semaphore_signal(barrier, inc=1, device_id=peer, device_id_type=pl.DeviceIdType.MESH)
    for copy in locals_:
        copy.wait()
    pl.semaphore_wait(barrier, 4 + len(peers))

    def block(slot, kind, target):
        return [
            pltpu.make_async_remote_copy(
                src_ref=buf.at[slot], dst_ref=buf.at[slot],
                send_sem=w_send.at[kind, n, slot], recv_sem=w_recv.at[n, slot],
                device_id=target, device_id_type=pl.DeviceIdType.MESH)
            for n, buf in enumerate((wbuf, lbuf))
        ]

    def start(slot, kind, target):
        for copy in block(slot, kind, target):
            copy.start()

    def arrive(slot):
        for copy in block(slot, 0, right1):
            copy.wait_recv()

    def sent(slot, kind):
        for copy in block(slot, kind, right1):
            copy.wait_send()

    def states(cc, xx, kind, target):
        xs = (xx + 2 * TENSORS) & (TENSORS - 1)
        return pltpu.make_async_remote_copy(
            src_ref=hbuf.at[cc, xs], dst_ref=hbuf.at[cc, xs],
            send_sem=h_send.at[kind, xs], recv_sem=h_recv.at[cc, xs],
            device_id=target, device_id_type=pl.DeviceIdType.MESH)

    codes = pltpu.make_async_remote_copy(
        src_ref=cbuf.at[core], dst_ref=cbuf.at[core], send_sem=c_sem.at[0], recv_sem=c_sem.at[1],
        device_id=partner, device_id_type=pl.DeviceIdType.MESH)
    way = 1 - 2 * core
    start(slot0, 0, right1)
    start(slot0, 1, left1)
    states(core, x, 0, at_x(x + 1, core)).start()
    states(core, x, 1, at_x(x - 1, core)).start()
    states(core, x, 3, partner).start()
    codes.start()
    start(slot0, 2, right2)
    start(slot0, 3, left2)

    def first(i):
        slot = q * RING + wrap(p + zigzag(i))
        arrive(slot)
        if i in (1, 3, 5):
            start(slot, 0, right1)
        if i in (2, 4):
            start(slot, 1, left1)
        start(slot, 2, right2)
        start(slot, 3, left2)

    for i in range(1, 4):
        first(i)
    for d in (-1, 1):
        states(core, x + d, 0, partner).wait_recv()
    states(core, x - way, 2, at_x(x + way, core)).start()
    for d in (-1, 1):
        states(core, x + d, 3, partner).start()
    for i in range(4, 8):
        first(i)

    def from_left(t, i, forward):
        slot = wrap(q - t) * RING + wrap(p + zigzag(i))
        arrive(slot)
        if forward:
            start(slot, 2, right2)

    def from_right(t, i, forward):
        slot = wrap(q + t) * RING + wrap(p + zigzag(i))
        arrive(slot)
        if forward:
            start(slot, 3, left2)

    def both(t, low, high):
        @pl.loop(low, high)
        def _(i):
            from_left(t, i, True)
            from_right(t, i, True)

    both(1, 0, 4)
    states(core, x + 2, 0, partner).wait_recv()
    states(core, x + 2, 3, partner).start()
    both(1, 4, 8)

    spots = lax.broadcasted_iota(jnp.int32, select.shape, 1)
    select[...] = jnp.where(spots == place_ref[...], 1.0, 0.0).astype(jnp.bfloat16)
    line_out[...] = jnp.zeros(line_out.shape, F32)

    for d in range(TENSORS):
        states(1 - core, x + d, 0, partner).wait_recv()
    codes.wait_recv()
    for c in range(2):
        power = jnp.zeros((1, rows), F32)
        for d in range(TENSORS):
            part = hbuf[c, d].astype(F32)
            power += jnp.sum(part * part, axis=0, keepdims=True)
        scale = lax.rsqrt(power / (TENSORS * feats) + 1e-06)
        for d in range(TENSORS):
            span = pl.ds(d * feats, feats)
            part = hbuf[c, d].astype(F32) * scale * gain_ref[span, :]
            normed[span, pl.ds(c * rows, rows)] = part.astype(jnp.bfloat16)
    stats[0] = jnp.full(stats.shape[1:], -1e30, F32)
    for n in range(1, 4):
        stats[n] = jnp.zeros(stats.shape[1:], F32)
    mine = (x * 2 + core) * 4096
    per = rows // CHUNK

    def update(weights, count, base, r):
        cols = pl.ds(pl.multiple_of(r * CHUNK, CHUNK), CHUNK)
        logits = jnp.dot(weights, normed[:, cols], preferred_element_type=F32)
        cube = logits.reshape(count // 8, 8, CHUNK)
        half = r // per
        span = pl.ds(pl.multiple_of((r - half * per) * CHUNK, CHUNK), CHUNK)
        wanted = cbuf[half, :, span] - (mine + base)
        ids = lax.broadcasted_iota(jnp.int32, (count, CHUNK), 0)
        old = stats[0, :, cols]
        top = jnp.maximum(old, jnp.max(cube, axis=0))
        factor = jnp.exp(old - top)
        weight = jnp.exp(cube - top[None])
        stats[0, :, cols] = top
        stats[1, :, cols] = stats[1, :, cols] * factor + jnp.sum(weight, axis=0)
        stats[2, :, cols] = stats[2, :, cols] * factor + jnp.sum(weight * cube, axis=0)
        hit = jnp.where(ids == wanted, logits, 0.0).reshape(count // 8, 8, CHUNK)
        stats[3, :, cols] = stats[3, :, cols] + jnp.sum(hit, axis=0)

    chunks = 2 * per

    def unit(u):
        k = u // chunks
        r = u - k * chunks
        g = wrap(q + zigzag(k))
        weights = wbuf[pl.ds(pl.multiple_of(g * RING, RING), RING)].reshape(RING * MAIN, -1)
        update(weights, RING * MAIN, g * (RING * MAIN), r)

    @pl.loop(0, 8)
    def _(i):
        from_left(2, i, True)
        from_right(2, i, True)
        unit(i)

    @pl.loop(0, 4)
    def _(i):
        from_left(3, i, True)
        from_right(3, i, False)
        unit(8 + i)

    @pl.loop(4, 8)
    def _(i):
        from_left(3, i, False)
        from_right(3, i, True)
        unit(8 + i)

    @pl.loop(0, 4)
    def _(i):
        from_left(4, i, False)
        unit(16 + 2 * i)
        from_right(4, i + 4, False)
        unit(17 + 2 * i)

    @pl.loop(24, 32)
    def _(u):
        unit(u)

    total = RING * RING * 2
    wide_rest[...] = lbuf[...].astype(F32).reshape(total * 8, 128)
    for k in range(8):
        rest[:, pl.ds(k * 128, 128)] = wide_rest[pl.ds(k, total, stride=8), :].astype(jnp.bfloat16)

    @pl.loop(0, chunks)
    def _(r):
        update(rest[...], total, RING * RING * MAIN, r)

    top = jnp.max(stats[0], axis=0, keepdims=True)
    factor = jnp.exp(stats[0] - top)
    lines = [top] + [jnp.sum(stats[n] * factor, axis=0, keepdims=True) for n in (1, 2)]
    lines.append(jnp.sum(stats[3], axis=0, keepdims=True))
    for c in range(2):
        for n, line in enumerate(lines):
            packed[c, pl.ds(n, 1), :] = line[:, c * rows:(c + 1) * rows]
        packed[c, pl.ds(4, 4), :] = jnp.zeros((4, rows), F32)
    who = x * 2 + core

    def result(n, peer):
        return pltpu.make_async_remote_copy(
            src_ref=packed.at[peer[2]], dst_ref=gath.at[who],
            send_sem=s_send.at[n], recv_sem=s_recv.at[who],
            device_id=peer, device_id_type=pl.DeviceIdType.MESH)

    def result_from(n, peer):
        source = peer[3] * 2 + peer[2]
        return pltpu.make_async_remote_copy(
            src_ref=packed.at[core], dst_ref=gath.at[source],
            send_sem=s_send.at[n], recv_sem=s_recv.at[source],
            device_id=peer, device_id_type=pl.DeviceIdType.MESH)

    for n, peer in enumerate(peers):
        result(n, peer).start()
    own = pltpu.make_async_copy(packed.at[core], gath.at[who], local_sem.at[0])
    own.start()

    own.wait()
    for n, peer in enumerate(peers):
        result_from(n, peer).wait_recv()

    tops = gath[:, 0, :]
    top = jnp.max(tops, axis=0, keepdims=True)
    factor = jnp.exp(tops - top)
    mass = jnp.sum(gath[:, 1, :] * factor, axis=0, keepdims=True)
    moment = jnp.sum(gath[:, 2, :] * factor, axis=0, keepdims=True)
    picked = jnp.sum(gath[:, 3, :], axis=0, keepdims=True)
    live = live_ref[...] > 0
    lse = top + jnp.log(mass)
    values[pl.ds(0, 1), :] = jnp.where(live, picked - lse, 0.0)
    values[pl.ds(1, 1), :] = jnp.where(live, lse - moment / mass, 0.0)
    exact = values[...]
    high = exact.astype(jnp.bfloat16)
    left = exact - high.astype(F32)
    middle = left.astype(jnp.bfloat16)
    low = (left - middle.astype(F32)).astype(jnp.bfloat16)
    ordered = jnp.zeros((2, select.shape[1]), F32)
    for term in (low, middle, high):
        ordered += jnp.dot(term, select[...], preferred_element_type=F32)
    for n in range(RING):
        line_out[n, pl.ds(0, 2), :] = ordered[:, n * 128:(n + 1) * 128]

    def along_line(d, other, source):
        return pltpu.make_async_remote_copy(
            src_ref=line_out.at[other], dst_ref=line_in.at[source],
            send_sem=l_send.at[d], recv_sem=l_recv.at[source],
            device_id=(other, y, core, x), device_id_type=pl.DeviceIdType.MESH)

    own_line = pltpu.make_async_copy(line_out.at[z], line_in.at[z], local_sem.at[1])
    for d in range(1, RING):
        along_line(d, wrap(z + d), z).start()
    own_line.start()
    own_line.wait()
    for d in range(1, RING):
        along_line(d, wrap(z + d), wrap(z + d)).wait_recv()
    first_half, second_half = line_in[:, 0, :], line_in[:, 1, :]
    lanes = lax.broadcasted_iota(jnp.int32, (RING, 128), 1)
    for n in range(2 * RING):
        plane_out[n] = jnp.where(
            lanes < 4, pltpu.roll(first_half, (128 - 4 * n) % 128, 1),
            pltpu.roll(second_half, (132 - 4 * n) % 128, 1))
    here = y * 2 + core

    def across_plane(d, other, source):
        return pltpu.make_async_remote_copy(
            src_ref=plane_out.at[other], dst_ref=plane_in.at[source],
            send_sem=p_send.at[d], recv_sem=p_recv.at[source],
            device_id=(z, other >> 1, other & 1, x), device_id_type=pl.DeviceIdType.MESH)

    def turn(d):
        return (here + d) & (2 * RING - 1)

    own_plane = pltpu.make_async_copy(plane_out.at[here], plane_in.at[here], local_sem.at[2])
    for d in range(1, 2 * RING):
        across_plane(d, turn(d), here).start()
    own_plane.start()

    for t in range(4):
        sent(q * RING + wrap(p - t), 0)
    for t in range(3):
        sent(q * RING + wrap(p + t), 1)

    @pl.loop(0, 8)
    def _(i):
        pp = wrap(p + zigzag(i))
        for t in range(3):
            sent(wrap(q - t) * RING + pp, 2)
            sent(wrap(q + t) * RING + pp, 3)

    @pl.loop(0, 4)
    def _(i):
        sent(wrap(q - 3) * RING + wrap(p + zigzag(i)), 2)
        sent(wrap(q + 3) * RING + wrap(p + zigzag(i + 4)), 3)

    states(core, x, 0, partner).wait_send()
    states(core, x, 1, partner).wait_send()
    states(core, x - way, 2, partner).wait_send()
    for d in range(TENSORS):
        states(core, x + d, 3, partner).wait_send()
    codes.wait_send()
    for n, peer in enumerate(peers):
        result(n, peer).wait_send()
    for d in range(1, RING):
        along_line(d, wrap(z + d), z).wait_send()
    own_plane.wait()
    for d in range(1, 2 * RING):
        across_plane(d, turn(d), here).wait_send()
        across_plane(d, turn(d), turn(d)).wait_recv()
    out_ref[...] = plane_in[...]


def head(main, rest, hid, code, gain, place, live):
    rows, feats, slots = hid.shape[1], hid.shape[0], RING * RING
    depth = TENSORS * feats
    any_space = pl.BlockSpec(memory_space=pl.ANY)
    vmem = pl.BlockSpec(memory_space=pltpu.VMEM)
    dma = pltpu.SemaphoreType.DMA
    return pl.pallas_call(
        head_kernel,
        out_shape=jax.ShapeDtypeStruct((2 * RING, RING, 128), F32),
        in_specs=[any_space] * 4 + [vmem] * 3,
        out_specs=vmem,
        scratch_shapes=[
            pltpu.VMEM((slots, MAIN, depth), jnp.bfloat16),
            pltpu.VMEM((slots, 16, 128), jnp.bfloat16),
            pltpu.VMEM((2, TENSORS, feats, rows), jnp.bfloat16),
            pltpu.VMEM((2, 1, rows), jnp.int32),
            pltpu.VMEM((depth, 2 * rows), jnp.bfloat16),
            pltpu.VMEM((slots * 16, 128), F32),
            pltpu.VMEM((slots * 2, depth), jnp.bfloat16),
            pltpu.VMEM((4, 8, 2 * rows), F32),
            pltpu.VMEM((2, 8, rows), F32),
            pltpu.VMEM((2 * TENSORS, 8, rows), F32),
            pltpu.VMEM((rows, RING * 128), jnp.bfloat16),
            pltpu.VMEM((2, rows), F32),
            pltpu.VMEM((RING, 8, 128), F32),
            pltpu.VMEM((RING, 8, 128), F32),
            pltpu.VMEM((2 * RING, RING, 128), F32),
            pltpu.VMEM((2 * RING, RING, 128), F32),
            dma((2, slots)), dma((4, 2, slots)), dma((2, TENSORS)), dma((4, TENSORS)),
            dma((2,)), dma((2 * TENSORS,)), dma((2 * TENSORS,)), dma((4,)),
            dma((RING,)), dma((RING,)), dma((2 * RING,)), dma((2 * RING,)),
        ],
        compiler_params=pltpu.CompilerParams(
            collective_id=0, has_side_effects=True, vmem_limit_bytes=48 << 20),
    )(main, rest, hid, code, gain, place, live)


def body(hidden, gain, head_weight, targets, row_count, dest):
    rows = hidden.shape[0]
    cols = head_weight.shape[1]
    groups = 2 * RING * RING
    turned = head_weight.T
    rest = turned[MAIN:].reshape(16, 128)
    owner, column = targets // (cols * groups), targets % cols
    device = (targets // cols) % groups
    near, zy = device % 2, device // 2
    zi, yi = zy // RING, zy % RING
    slot = jnp.where(near == 0, yi * RING + zi, zi * RING + yi)
    index = jnp.where(column < MAIN, slot * MAIN + column, RING * RING * MAIN + slot * 2 + column - MAIN)
    code = ((owner * 2 + near) * 4096 + index).reshape(1, rows)
    share = rows // groups
    rank = (dest // rows) * share + dest % share
    line = rows // RING
    place = (rank // line) * 128 + rank % line
    live = (jnp.arange(rows, dtype=jnp.int32) < row_count[0]).astype(jnp.int32)
    got = head(turned, rest, hidden.T, code, gain.reshape(-1, 1), place.reshape(-1, 1), live.reshape(1, -1))
    got = jnp.moveaxis(got[:, :, :2 * share], 1, 0)
    return got[:, :, :share].reshape(rows), got[:, :, share:].reshape(rows)


def solution(mesh):
    tensor = mesh.devices.shape[1]
    fine = Mesh(mesh.devices.reshape(RING, RING, 2, tensor), ("z", "y", "core", "tensor"))
    group = ("z", "y", "core")
    in_specs = (P(group, "tensor"), P(), P(None, ("tensor", "z", "y", "core")), P(group), P(group), P(group))
    return jax.shard_map(body, mesh=fine, in_specs=in_specs, out_specs=(P(group), P(group)), check_vma=False)
```

```python
import functools

import jax
import jax.numpy as jnp
from jax import lax
from jax.experimental import pallas as pl
from jax.experimental.pallas import tpu as pltpu
from jax.sharding import Mesh, PartitionSpec as P

RING = 8
TENSORS = 4
MAIN = 48
CHUNK = 256
F32 = jnp.float32


def zigzag(i):
    return ((i + 1) >> 1) * (1 - 2 * (i & 1))


def head_kernel(main_hbm, rest_hbm, hid_hbm, code_hbm, gain_ref, place_ref, live_ref, out_ref,
                wbuf, lbuf, hbuf, cbuf, normed, wide_rest, rest, stats, packed, gath,
                select, values, line_out, line_in, plane_out, plane_in,
                b_recv, b_send, m_recv, m_send, r_recv, r_send, h_recv, h_send, c_sem, s_recv, s_send, local_sem,
                l_recv, l_send, p_recv, p_send):
    z, y = lax.axis_index("z"), lax.axis_index("y")
    core, x = lax.axis_index("core"), lax.axis_index("tensor")
    rows = hid_hbm.shape[1]
    feats = hid_hbm.shape[0]
    p = z + core * (y - z)
    q = y + core * (z - y)

    def wrap(v):
        return (v + 2 * RING) & (RING - 1)

    def at(pp, qq):
        return (pp + core * (qq - pp), qq + core * (pp - qq), core, x)

    def at_x(xx, cc):
        return (z, y, cc, (xx + 2 * TENSORS) & (TENSORS - 1))

    right1, left1 = at(wrap(p + 1), q), at(wrap(p - 1), q)
    right2, left2 = at(p, wrap(q + 1)), at(p, wrap(q - 1))
    partner = at_x(x, 1 - core)
    slot0 = q * RING

    locals_ = [
        pltpu.make_async_copy(main_hbm.at[pl.ds(0, MAIN)], wbuf.at[slot0], local_sem.at[0]),
        pltpu.make_async_copy(rest_hbm, lbuf.at[slot0], local_sem.at[1]),
        pltpu.make_async_copy(hid_hbm, hbuf.at[core, x], local_sem.at[2]),
        pltpu.make_async_copy(code_hbm, cbuf.at[core], local_sem.at[3]),
    ]
    for copy in locals_:
        copy.start()
    barrier = pltpu.get_barrier_semaphore()
    peers = [at_x(x + d, c) for d in range(TENSORS) for c in (core, 1 - core)][1:]
    for peer in [right1, left1, right2, left2] + peers:
        pl.semaphore_signal(barrier, inc=1, device_id=peer, device_id_type=pl.DeviceIdType.MESH)
    for copy in locals_:
        copy.wait()
    pl.semaphore_wait(barrier, 4 + len(peers))

    def block(index, landing, kind, target):
        return [
            pltpu.make_async_remote_copy(
                src_ref=buf.at[slot0 + index], dst_ref=buf.at[slot0 + landing],
                send_sem=b_send.at[kind, n, index], recv_sem=b_recv.at[n, landing],
                device_id=target, device_id_type=pl.DeviceIdType.MESH)
            for n, buf in enumerate((wbuf, lbuf))
        ]

    def message(group, half, kind, target):
        part = wbuf.at[pl.ds(group * RING + half * 4, 4)]
        return pltpu.make_async_remote_copy(
            src_ref=part, dst_ref=part,
            send_sem=m_send.at[kind, group, half], recv_sem=m_recv.at[group, half],
            device_id=target, device_id_type=pl.DeviceIdType.MESH)

    def remainder(group, kind, target):
        part = lbuf.at[pl.ds(group * RING, RING)]
        return pltpu.make_async_remote_copy(
            src_ref=part, dst_ref=part,
            send_sem=r_send.at[kind, group], recv_sem=r_recv.at[group],
            device_id=target, device_id_type=pl.DeviceIdType.MESH)

    def states(cc, xx, kind, target):
        xs = (xx + 2 * TENSORS) & (TENSORS - 1)
        return pltpu.make_async_remote_copy(
            src_ref=hbuf.at[cc, xs], dst_ref=hbuf.at[cc, xs],
            send_sem=h_send.at[kind, xs], recv_sem=h_recv.at[cc, xs],
            device_id=target, device_id_type=pl.DeviceIdType.MESH)

    codes = pltpu.make_async_remote_copy(
        src_ref=cbuf.at[core], dst_ref=cbuf.at[core], send_sem=c_sem.at[0], recv_sem=c_sem.at[1],
        device_id=partner, device_id_type=pl.DeviceIdType.MESH)
    way = 1 - 2 * core
    for copy in block(0, 1, 0, right1) + block(0, 2, 1, left1):
        copy.start()
    states(core, x, 0, at_x(x + 1, core)).start()
    states(core, x, 1, at_x(x - 1, core)).start()
    states(core, x, 3, partner).start()
    codes.start()

    def first(i):
        for copy in block(i, i, 0, right1):
            copy.wait_recv()
        onward = []
        if i in (1, 3, 5):
            onward = block(i, i + 2, 0, right1)
        if i in (2, 4):
            onward = block(i, i + 2, 1, left1)
        for copy in onward:
            copy.start()

    for i in range(1, 4):
        first(i)
    message(q, 0, 0, right2).start()
    message(q, 0, 1, left2).start()
    for d in (-1, 1):
        states(core, x + d, 0, partner).wait_recv()
    states(core, x - way, 2, at_x(x + way, core)).start()
    for d in (-1, 1):
        states(core, x + d, 3, partner).start()
    for i in range(4, 8):
        first(i)

    remainder(q, 0, right2).start()
    remainder(q, 1, left2).start()
    message(q, 1, 0, right2).start()
    message(q, 1, 1, left2).start()

    def second(t, half):
        back, ahead = wrap(q - t), wrap(q + t)
        if half == 1:
            remainder(back, 0, right2).wait_recv()
            if t < 4:
                remainder(back, 0, right2).start()
                remainder(ahead, 1, left2).wait_recv()
            if t < 3:
                remainder(ahead, 1, left2).start()
        if t < 4 or half == 0:
            message(back, half, 0, right2).wait_recv()
        if t < 3 or (t == 3 and half == 0):
            message(back, half, 0, right2).start()
        if t < 4 or half == 1:
            message(ahead, half, 1, left2).wait_recv()
        if t < 3 or (t == 3 and half == 1):
            message(ahead, half, 1, left2).start()

    spots = lax.broadcasted_iota(jnp.int32, select.shape, 1)
    select[...] = jnp.where(spots == place_ref[...], 1.0, 0.0).astype(jnp.bfloat16)
    line_out[...] = jnp.zeros(line_out.shape, F32)
    states(core, x + 2, 0, partner).wait_recv()
    states(core, x + 2, 3, partner).start()
    second(1, 0)

    for d in range(TENSORS):
        states(1 - core, x + d, 0, partner).wait_recv()
    codes.wait_recv()
    for c in range(2):
        power = jnp.zeros((1, rows), F32)
        for d in range(TENSORS):
            part = hbuf[c, d].astype(F32)
            power += jnp.sum(part * part, axis=0, keepdims=True)
        scale = lax.rsqrt(power / (TENSORS * feats) + 1e-06)
        for d in range(TENSORS):
            span = pl.ds(d * feats, feats)
            part = hbuf[c, d].astype(F32) * scale * gain_ref[span, :]
            normed[span, pl.ds(c * rows, rows)] = part.astype(jnp.bfloat16)
    stats[0] = jnp.full(stats.shape[1:], -1e30, F32)
    for n in range(1, 4):
        stats[n] = jnp.zeros(stats.shape[1:], F32)
    mine = (x * 2 + core) * 4096
    per = rows // CHUNK

    def update(weights, count, base, r):
        cols = pl.ds(pl.multiple_of(r * CHUNK, CHUNK), CHUNK)
        logits = jnp.dot(weights, normed[:, cols], preferred_element_type=F32)
        cube = logits.reshape(count // 8, 8, CHUNK)
        half = r // per
        span = pl.ds(pl.multiple_of((r - half * per) * CHUNK, CHUNK), CHUNK)
        wanted = cbuf[half, :, span] - (mine + base)
        ids = lax.broadcasted_iota(jnp.int32, (count, CHUNK), 0)
        old = stats[0, :, cols]
        top = jnp.maximum(old, jnp.max(cube, axis=0))
        factor = jnp.exp(old - top)
        weight = jnp.exp(cube - top[None])
        stats[0, :, cols] = top
        stats[1, :, cols] = stats[1, :, cols] * factor + jnp.sum(weight, axis=0)
        stats[2, :, cols] = stats[2, :, cols] * factor + jnp.sum(weight * cube, axis=0)
        hit = jnp.where(ids == wanted, logits, 0.0).reshape(count // 8, 8, CHUNK)
        stats[3, :, cols] = stats[3, :, cols] + jnp.sum(hit, axis=0)

    chunks = 2 * per

    def unit(u):
        k = u // chunks
        r = u - k * chunks
        g = wrap(q + zigzag(k))
        weights = wbuf[pl.ds(pl.multiple_of(g * RING, RING), RING)].reshape(RING * MAIN, -1)
        update(weights, RING * MAIN, g * (RING * MAIN), r)

    def units(low, high):
        @pl.loop(low, high)
        def _(u):
            unit(u)

    second(1, 1)
    units(0, 4)
    second(2, 0)
    units(4, 8)
    second(2, 1)
    units(8, 12)
    second(3, 0)
    units(12, 16)
    second(3, 1)
    units(16, 28)
    second(4, 0)
    second(4, 1)
    units(28, 32)

    total = RING * RING * 2
    wide_rest[...] = lbuf[...].astype(F32).reshape(total * 8, 128)
    for k in range(8):
        rest[:, pl.ds(k * 128, 128)] = wide_rest[pl.ds(k, total, stride=8), :].astype(jnp.bfloat16)

    @pl.loop(0, chunks)
    def _(r):
        update(rest[...], total, RING * RING * MAIN, r)

    top = jnp.max(stats[0], axis=0, keepdims=True)
    factor = jnp.exp(stats[0] - top)
    lines = [top] + [jnp.sum(stats[n] * factor, axis=0, keepdims=True) for n in (1, 2)]
    lines.append(jnp.sum(stats[3], axis=0, keepdims=True))
    for c in range(2):
        for n, line in enumerate(lines):
            packed[c, pl.ds(n, 1), :] = line[:, c * rows:(c + 1) * rows]
        packed[c, pl.ds(4, 4), :] = jnp.zeros((4, rows), F32)
    who = x * 2 + core

    def result(n, peer):
        return pltpu.make_async_remote_copy(
            src_ref=packed.at[peer[2]], dst_ref=gath.at[who],
            send_sem=s_send.at[n], recv_sem=s_recv.at[who],
            device_id=peer, device_id_type=pl.DeviceIdType.MESH)

    def result_from(n, peer):
        source = peer[3] * 2 + peer[2]
        return pltpu.make_async_remote_copy(
            src_ref=packed.at[core], dst_ref=gath.at[source],
            send_sem=s_send.at[n], recv_sem=s_recv.at[source],
            device_id=peer, device_id_type=pl.DeviceIdType.MESH)

    for n, peer in enumerate(peers):
        result(n, peer).start()
    own = pltpu.make_async_copy(packed.at[core], gath.at[who], local_sem.at[0])
    own.start()

    own.wait()
    for n, peer in enumerate(peers):
        result_from(n, peer).wait_recv()

    tops = gath[:, 0, :]
    top = jnp.max(tops, axis=0, keepdims=True)
    factor = jnp.exp(tops - top)
    mass = jnp.sum(gath[:, 1, :] * factor, axis=0, keepdims=True)
    moment = jnp.sum(gath[:, 2, :] * factor, axis=0, keepdims=True)
    picked = jnp.sum(gath[:, 3, :], axis=0, keepdims=True)
    live = live_ref[...] > 0
    lse = top + jnp.log(mass)
    values[pl.ds(0, 1), :] = jnp.where(live, picked - lse, 0.0)
    values[pl.ds(1, 1), :] = jnp.where(live, lse - moment / mass, 0.0)
    exact = values[...]
    high = exact.astype(jnp.bfloat16)
    left = exact - high.astype(F32)
    middle = left.astype(jnp.bfloat16)
    low = (left - middle.astype(F32)).astype(jnp.bfloat16)
    ordered = jnp.zeros((2, select.shape[1]), F32)
    for term in (low, middle, high):
        ordered += jnp.dot(term, select[...], preferred_element_type=F32)
    for n in range(RING):
        line_out[n, pl.ds(0, 2), :] = ordered[:, n * 128:(n + 1) * 128]

    def along_line(d, other, source):
        return pltpu.make_async_remote_copy(
            src_ref=line_out.at[other], dst_ref=line_in.at[source],
            send_sem=l_send.at[d], recv_sem=l_recv.at[source],
            device_id=(other, y, core, x), device_id_type=pl.DeviceIdType.MESH)

    own_line = pltpu.make_async_copy(line_out.at[z], line_in.at[z], local_sem.at[1])
    for d in range(1, RING):
        along_line(d, wrap(z + d), z).start()
    own_line.start()
    own_line.wait()
    for d in range(1, RING):
        along_line(d, wrap(z + d), wrap(z + d)).wait_recv()
    first_half, second_half = line_in[:, 0, :], line_in[:, 1, :]
    lanes = lax.broadcasted_iota(jnp.int32, (RING, 128), 1)
    for n in range(2 * RING):
        plane_out[n] = jnp.where(
            lanes < 4, pltpu.roll(first_half, (128 - 4 * n) % 128, 1),
            pltpu.roll(second_half, (132 - 4 * n) % 128, 1))
    here = y * 2 + core

    def across_plane(d, other, source):
        return pltpu.make_async_remote_copy(
            src_ref=plane_out.at[other], dst_ref=plane_in.at[source],
            send_sem=p_send.at[d], recv_sem=p_recv.at[source],
            device_id=(z, other >> 1, other & 1, x), device_id_type=pl.DeviceIdType.MESH)

    def turn(d):
        return (here + d) & (2 * RING - 1)

    own_plane = pltpu.make_async_copy(plane_out.at[here], plane_in.at[here], local_sem.at[2])
    for d in range(1, 2 * RING):
        across_plane(d, turn(d), here).start()
    own_plane.start()

    for i in (0, 1, 3, 5):
        for copy in block(i, i, 0, right1):
            copy.wait_send()
    for i in (0, 2, 4):
        for copy in block(i, i, 1, left1):
            copy.wait_send()
    for t in range(4):
        back, ahead = wrap(q - t), wrap(q + t)
        remainder(back, 0, right2).wait_send()
        message(back, 0, 0, right2).wait_send()
        message(ahead, 1, 1, left2).wait_send()
        if t < 3:
            remainder(ahead, 1, left2).wait_send()
            message(back, 1, 0, right2).wait_send()
            message(ahead, 0, 1, left2).wait_send()

    states(core, x, 0, partner).wait_send()
    states(core, x, 1, partner).wait_send()
    states(core, x - way, 2, partner).wait_send()
    for d in range(TENSORS):
        states(core, x + d, 3, partner).wait_send()
    codes.wait_send()
    for n, peer in enumerate(peers):
        result(n, peer).wait_send()
    for d in range(1, RING):
        along_line(d, wrap(z + d), z).wait_send()
    own_plane.wait()
    for d in range(1, 2 * RING):
        across_plane(d, turn(d), here).wait_send()
        across_plane(d, turn(d), turn(d)).wait_recv()
    out_ref[...] = plane_in[...]


def head(main, rest, hid, code, gain, place, live):
    rows, feats, slots = hid.shape[1], hid.shape[0], RING * RING
    depth = TENSORS * feats
    any_space = pl.BlockSpec(memory_space=pl.ANY)
    vmem = pl.BlockSpec(memory_space=pltpu.VMEM)
    dma = pltpu.SemaphoreType.DMA
    return pl.pallas_call(
        head_kernel,
        out_shape=jax.ShapeDtypeStruct((2 * RING, RING, 128), F32),
        in_specs=[any_space] * 4 + [vmem] * 3,
        out_specs=vmem,
        scratch_shapes=[
            pltpu.VMEM((slots, MAIN, depth), jnp.bfloat16),
            pltpu.VMEM((slots, 16, 128), jnp.bfloat16),
            pltpu.VMEM((2, TENSORS, feats, rows), jnp.bfloat16),
            pltpu.VMEM((2, 1, rows), jnp.int32),
            pltpu.VMEM((depth, 2 * rows), jnp.bfloat16),
            pltpu.VMEM((slots * 16, 128), F32),
            pltpu.VMEM((slots * 2, depth), jnp.bfloat16),
            pltpu.VMEM((4, 8, 2 * rows), F32),
            pltpu.VMEM((2, 8, rows), F32),
            pltpu.VMEM((2 * TENSORS, 8, rows), F32),
            pltpu.VMEM((rows, RING * 128), jnp.bfloat16),
            pltpu.VMEM((2, rows), F32),
            pltpu.VMEM((RING, 8, 128), F32),
            pltpu.VMEM((RING, 8, 128), F32),
            pltpu.VMEM((2 * RING, RING, 128), F32),
            pltpu.VMEM((2 * RING, RING, 128), F32),
            dma((2, RING)), dma((2, 2, RING)), dma((RING, 2)), dma((2, RING, 2)), dma((RING,)), dma((2, RING)),
            dma((2, TENSORS)), dma((4, TENSORS)),
            dma((2,)), dma((2 * TENSORS,)), dma((2 * TENSORS,)), dma((4,)),
            dma((RING,)), dma((RING,)), dma((2 * RING,)), dma((2 * RING,)),
        ],
        compiler_params=pltpu.CompilerParams(
            collective_id=0, has_side_effects=True, vmem_limit_bytes=48 << 20),
    )(main, rest, hid, code, gain, place, live)


def body(hidden, gain, head_weight, targets, row_count, dest):
    rows = hidden.shape[0]
    cols = head_weight.shape[1]
    groups = 2 * RING * RING
    turned = head_weight.T
    rest = turned[MAIN:].reshape(16, 128)
    owner, column = targets // (cols * groups), targets % cols
    device = (targets // cols) % groups
    near, zy = device % 2, device // 2
    zi, yi = zy // RING, zy % RING
    z, y = lax.axis_index("z"), lax.axis_index("y")
    gone = (jnp.where(near == 0, zi - z, yi - y) + RING) % RING
    order = jnp.where(gone < RING // 2, 2 * gone, 2 * (RING - gone) - 1)
    slot = jnp.where(near == 0, yi, zi) * RING + order
    index = jnp.where(column < MAIN, slot * MAIN + column, RING * RING * MAIN + slot * 2 + column - MAIN)
    code = ((owner * 2 + near) * 4096 + index).reshape(1, rows)
    share = rows // groups
    rank = (dest // rows) * share + dest % share
    line = rows // RING
    place = (rank // line) * 128 + rank % line
    live = (jnp.arange(rows, dtype=jnp.int32) < row_count[0]).astype(jnp.int32)
    got = head(turned, rest, hidden.T, code, gain.reshape(-1, 1), place.reshape(-1, 1), live.reshape(1, -1))
    got = jnp.moveaxis(got[:, :, :2 * share], 1, 0)
    return got[:, :, :share].reshape(rows), got[:, :, share:].reshape(rows)


def solution(mesh):
    tensor = mesh.devices.shape[1]
    fine = Mesh(mesh.devices.reshape(RING, RING, 2, tensor), ("z", "y", "core", "tensor"))
    group = ("z", "y", "core")
    in_specs = (P(group, "tensor"), P(), P(None, ("tensor", "z", "y", "core")), P(group), P(group), P(group))
    return jax.shard_map(body, mesh=fine, in_specs=in_specs, out_specs=(P(group), P(group)), check_vma=False)
```

```python
import functools

import jax
import jax.numpy as jnp
from jax import lax
from jax.experimental import pallas as pl
from jax.experimental.pallas import tpu as pltpu
from jax.sharding import Mesh, PartitionSpec as P

RING = 8
TENSORS = 4
MAIN = 48
CHUNK = 256
F32 = jnp.float32


def zigzag(i):
    return ((i + 1) >> 1) * (1 - 2 * (i & 1))


def head_kernel(main_hbm, rest_hbm, hid_hbm, code_hbm, gain_ref, place_ref, live_ref, out_ref,
                wbuf, lbuf, hbuf, cbuf, normed, wide_rest, rest, stats, packed, gath,
                select, values, line_out, line_in, plane_out, plane_in,
                b_recv, b_send, m_recv, m_send, o_recv, o_send, r_recv, r_send, h_recv, h_send, c_sem, s_recv, s_send, local_sem,
                l_recv, l_send, p_recv, p_send):
    z, y = lax.axis_index("z"), lax.axis_index("y")
    core, x = lax.axis_index("core"), lax.axis_index("tensor")
    rows = hid_hbm.shape[1]
    feats = hid_hbm.shape[0]
    p = z + core * (y - z)
    q = y + core * (z - y)

    def wrap(v):
        return (v + 2 * RING) & (RING - 1)

    def at(pp, qq):
        return (pp + core * (qq - pp), qq + core * (pp - qq), core, x)

    def at_x(xx, cc):
        return (z, y, cc, (xx + 2 * TENSORS) & (TENSORS - 1))

    right1, left1 = at(wrap(p + 1), q), at(wrap(p - 1), q)
    right2, left2 = at(p, wrap(q + 1)), at(p, wrap(q - 1))
    partner = at_x(x, 1 - core)
    slot0 = q * RING

    locals_ = [
        pltpu.make_async_copy(main_hbm.at[pl.ds(0, MAIN)], wbuf.at[slot0], local_sem.at[0]),
        pltpu.make_async_copy(rest_hbm, lbuf.at[slot0], local_sem.at[1]),
        pltpu.make_async_copy(hid_hbm, hbuf.at[core, x], local_sem.at[2]),
        pltpu.make_async_copy(code_hbm, cbuf.at[core], local_sem.at[3]),
    ]
    for copy in locals_:
        copy.start()
    barrier = pltpu.get_barrier_semaphore()
    peers = [at_x(x + d, c) for d in range(TENSORS) for c in (core, 1 - core)][1:]
    for peer in [right1, left1, right2, left2] + peers:
        pl.semaphore_signal(barrier, inc=1, device_id=peer, device_id_type=pl.DeviceIdType.MESH)
    for copy in locals_:
        copy.wait()
    pl.semaphore_wait(barrier, 4 + len(peers))

    def block(index, landing, kind, target):
        return [
            pltpu.make_async_remote_copy(
                src_ref=buf.at[slot0 + index], dst_ref=buf.at[slot0 + landing],
                send_sem=b_send.at[kind, n, index], recv_sem=b_recv.at[n, landing],
                device_id=target, device_id_type=pl.DeviceIdType.MESH)
            for n, buf in enumerate((wbuf, lbuf))
        ]

    def message(group, half, kind, target):
        part = wbuf.at[pl.ds(group * RING + half * 4, 4)]
        return pltpu.make_async_remote_copy(
            src_ref=part, dst_ref=part,
            send_sem=m_send.at[kind, group, half], recv_sem=m_recv.at[group, half],
            device_id=target, device_id_type=pl.DeviceIdType.MESH)

    def single(group, index, kind, target):
        part = wbuf.at[group * RING + index]
        return pltpu.make_async_remote_copy(
            src_ref=part, dst_ref=part,
            send_sem=o_send.at[kind, index], recv_sem=o_recv.at[kind, index],
            device_id=target, device_id_type=pl.DeviceIdType.MESH)

    def remainder(group, kind, target):
        part = lbuf.at[pl.ds(group * RING, RING)]
        return pltpu.make_async_remote_copy(
            src_ref=part, dst_ref=part,
            send_sem=r_send.at[kind, group], recv_sem=r_recv.at[group],
            device_id=target, device_id_type=pl.DeviceIdType.MESH)

    def states(cc, xx, kind, target):
        xs = (xx + 2 * TENSORS) & (TENSORS - 1)
        return pltpu.make_async_remote_copy(
            src_ref=hbuf.at[cc, xs], dst_ref=hbuf.at[cc, xs],
            send_sem=h_send.at[kind, xs], recv_sem=h_recv.at[cc, xs],
            device_id=target, device_id_type=pl.DeviceIdType.MESH)

    codes = pltpu.make_async_remote_copy(
        src_ref=cbuf.at[core], dst_ref=cbuf.at[core], send_sem=c_sem.at[0], recv_sem=c_sem.at[1],
        device_id=partner, device_id_type=pl.DeviceIdType.MESH)
    way = 1 - 2 * core
    for copy in block(0, 1, 0, right1) + block(0, 2, 1, left1):
        copy.start()
    single(q, 0, 0, right2).start()
    single(q, 0, 1, left2).start()
    states(core, x, 0, at_x(x + 1, core)).start()
    states(core, x, 1, at_x(x - 1, core)).start()
    states(core, x, 3, partner).start()
    codes.start()

    def first(i):
        for copy in block(i, i, 0, right1):
            copy.wait_recv()
        onward = []
        if i in (1, 3, 5):
            onward = block(i, i + 2, 0, right1)
        if i in (2, 4):
            onward = block(i, i + 2, 1, left1)
        for copy in onward:
            copy.start()
        single(q, i, 0, right2).start()
        single(q, i, 1, left2).start()

    for i in range(1, 4):
        first(i)
    for d in (-1, 1):
        states(core, x + d, 0, partner).wait_recv()
    states(core, x - way, 2, at_x(x + way, core)).start()
    for d in (-1, 1):
        states(core, x + d, 3, partner).start()
    for i in range(4, 8):
        first(i)

    remainder(q, 0, right2).start()
    remainder(q, 1, left2).start()

    def second(t, half):
        back, ahead = wrap(q - t), wrap(q + t)
        if half == 1:
            remainder(back, 0, right2).wait_recv()
            if t < 4:
                remainder(back, 0, right2).start()
                remainder(ahead, 1, left2).wait_recv()
            if t < 3:
                remainder(ahead, 1, left2).start()
        if t == 1:
            for index in range(4 * half, 4 * half + 4):
                single(back, index, 0, right2).wait_recv()
        elif t < 4 or half == 0:
            message(back, half, 0, right2).wait_recv()
        if t < 3 or (t == 3 and half == 0):
            message(back, half, 0, right2).start()
        if t == 1:
            for index in range(4 * half, 4 * half + 4):
                single(ahead, index, 1, left2).wait_recv()
        elif t < 4 or half == 1:
            message(ahead, half, 1, left2).wait_recv()
        if t < 3 or (t == 3 and half == 1):
            message(ahead, half, 1, left2).start()

    states(core, x + 2, 0, partner).wait_recv()
    states(core, x + 2, 3, partner).start()
    second(1, 0)
    spots = lax.broadcasted_iota(jnp.int32, select.shape, 1)
    select[...] = jnp.where(spots == place_ref[...], 1.0, 0.0).astype(jnp.bfloat16)
    line_out[...] = jnp.zeros(line_out.shape, F32)
    second(1, 1)

    for d in range(TENSORS):
        states(1 - core, x + d, 0, partner).wait_recv()
    codes.wait_recv()
    for c in range(2):
        power = jnp.zeros((1, rows), F32)
        for d in range(TENSORS):
            part = hbuf[c, d].astype(F32)
            power += jnp.sum(part * part, axis=0, keepdims=True)
        scale = lax.rsqrt(power / (TENSORS * feats) + 1e-06)
        for d in range(TENSORS):
            span = pl.ds(d * feats, feats)
            part = hbuf[c, d].astype(F32) * scale * gain_ref[span, :]
            normed[span, pl.ds(c * rows, rows)] = part.astype(jnp.bfloat16)
    stats[0] = jnp.full(stats.shape[1:], -1e30, F32)
    for n in range(1, 4):
        stats[n] = jnp.zeros(stats.shape[1:], F32)
    mine = (x * 2 + core) * 4096
    per = rows // CHUNK

    def update(weights, count, base, r):
        cols = pl.ds(pl.multiple_of(r * CHUNK, CHUNK), CHUNK)
        logits = jnp.dot(weights, normed[:, cols], preferred_element_type=F32)
        cube = logits.reshape(count // 8, 8, CHUNK)
        half = r // per
        span = pl.ds(pl.multiple_of((r - half * per) * CHUNK, CHUNK), CHUNK)
        wanted = cbuf[half, :, span] - (mine + base)
        ids = lax.broadcasted_iota(jnp.int32, (count, CHUNK), 0)
        old = stats[0, :, cols]
        top = jnp.maximum(old, jnp.max(cube, axis=0))
        factor = jnp.exp(old - top)
        weight = jnp.exp(cube - top[None])
        stats[0, :, cols] = top
        stats[1, :, cols] = stats[1, :, cols] * factor + jnp.sum(weight, axis=0)
        stats[2, :, cols] = stats[2, :, cols] * factor + jnp.sum(weight * cube, axis=0)
        hit = jnp.where(ids == wanted, logits, 0.0).reshape(count // 8, 8, CHUNK)
        stats[3, :, cols] = stats[3, :, cols] + jnp.sum(hit, axis=0)

    chunks = 2 * per

    def unit(u):
        k = u // chunks
        r = u - k * chunks
        g = wrap(q + zigzag(k))
        weights = wbuf[pl.ds(pl.multiple_of(g * RING, RING), RING)].reshape(RING * MAIN, -1)
        update(weights, RING * MAIN, g * (RING * MAIN), r)

    def units(low, high):
        @pl.loop(low, high)
        def _(u):
            unit(u)

    second(2, 0)
    units(0, 4)
    units(4, 8)
    second(2, 1)
    units(8, 12)
    second(3, 0)
    units(12, 16)
    second(3, 1)
    units(16, 28)
    second(4, 0)
    second(4, 1)
    units(28, 32)

    total = RING * RING * 2
    wide_rest[...] = lbuf[...].astype(F32).reshape(total * 8, 128)
    for k in range(8):
        rest[:, pl.ds(k * 128, 128)] = wide_rest[pl.ds(k, total, stride=8), :].astype(jnp.bfloat16)

    @pl.loop(0, chunks)
    def _(r):
        update(rest[...], total, RING * RING * MAIN, r)

    top = jnp.max(stats[0], axis=0, keepdims=True)
    factor = jnp.exp(stats[0] - top)
    lines = [top] + [jnp.sum(stats[n] * factor, axis=0, keepdims=True) for n in (1, 2)]
    lines.append(jnp.sum(stats[3], axis=0, keepdims=True))
    for c in range(2):
        for n, line in enumerate(lines):
            packed[c, pl.ds(n, 1), :] = line[:, c * rows:(c + 1) * rows]
        packed[c, pl.ds(4, 4), :] = jnp.zeros((4, rows), F32)
    who = x * 2 + core

    def result(n, peer):
        return pltpu.make_async_remote_copy(
            src_ref=packed.at[peer[2]], dst_ref=gath.at[who],
            send_sem=s_send.at[n], recv_sem=s_recv.at[who],
            device_id=peer, device_id_type=pl.DeviceIdType.MESH)

    def result_from(n, peer):
        source = peer[3] * 2 + peer[2]
        return pltpu.make_async_remote_copy(
            src_ref=packed.at[core], dst_ref=gath.at[source],
            send_sem=s_send.at[n], recv_sem=s_recv.at[source],
            device_id=peer, device_id_type=pl.DeviceIdType.MESH)

    for n, peer in enumerate(peers):
        result(n, peer).start()
    own = pltpu.make_async_copy(packed.at[core], gath.at[who], local_sem.at[0])
    own.start()

    own.wait()
    for n, peer in enumerate(peers):
        result_from(n, peer).wait_recv()

    tops = gath[:, 0, :]
    top = jnp.max(tops, axis=0, keepdims=True)
    factor = jnp.exp(tops - top)
    mass = jnp.sum(gath[:, 1, :] * factor, axis=0, keepdims=True)
    moment = jnp.sum(gath[:, 2, :] * factor, axis=0, keepdims=True)
    picked = jnp.sum(gath[:, 3, :], axis=0, keepdims=True)
    live = live_ref[...] > 0
    lse = top + jnp.log(mass)
    values[pl.ds(0, 1), :] = jnp.where(live, picked - lse, 0.0)
    values[pl.ds(1, 1), :] = jnp.where(live, lse - moment / mass, 0.0)
    exact = values[...]
    high = exact.astype(jnp.bfloat16)
    left = exact - high.astype(F32)
    middle = left.astype(jnp.bfloat16)
    low = (left - middle.astype(F32)).astype(jnp.bfloat16)
    ordered = jnp.zeros((2, select.shape[1]), F32)
    for term in (low, middle, high):
        ordered += jnp.dot(term, select[...], preferred_element_type=F32)
    for n in range(RING):
        line_out[n, pl.ds(0, 2), :] = ordered[:, n * 128:(n + 1) * 128]

    def along_line(d, other, source):
        return pltpu.make_async_remote_copy(
            src_ref=line_out.at[other], dst_ref=line_in.at[source],
            send_sem=l_send.at[d], recv_sem=l_recv.at[source],
            device_id=(other, y, core, x), device_id_type=pl.DeviceIdType.MESH)

    own_line = pltpu.make_async_copy(line_out.at[z], line_in.at[z], local_sem.at[1])
    for d in range(1, RING):
        along_line(d, wrap(z + d), z).start()
    own_line.start()
    own_line.wait()
    for d in range(1, RING):
        along_line(d, wrap(z + d), wrap(z + d)).wait_recv()
    first_half, second_half = line_in[:, 0, :], line_in[:, 1, :]
    lanes = lax.broadcasted_iota(jnp.int32, (RING, 128), 1)
    for n in range(2 * RING):
        plane_out[n] = jnp.where(
            lanes < 4, pltpu.roll(first_half, (128 - 4 * n) % 128, 1),
            pltpu.roll(second_half, (132 - 4 * n) % 128, 1))
    here = y * 2 + core

    def across_plane(d, other, source):
        return pltpu.make_async_remote_copy(
            src_ref=plane_out.at[other], dst_ref=plane_in.at[source],
            send_sem=p_send.at[d], recv_sem=p_recv.at[source],
            device_id=(z, other >> 1, other & 1, x), device_id_type=pl.DeviceIdType.MESH)

    def turn(d):
        return (here + d) & (2 * RING - 1)

    own_plane = pltpu.make_async_copy(plane_out.at[here], plane_in.at[here], local_sem.at[2])
    for d in range(1, 2 * RING):
        across_plane(d, turn(d), here).start()
    own_plane.start()

    for i in (0, 1, 3, 5):
        for copy in block(i, i, 0, right1):
            copy.wait_send()
    for i in (0, 2, 4):
        for copy in block(i, i, 1, left1):
            copy.wait_send()
    for index in range(RING):
        single(q, index, 0, right2).wait_send()
        single(q, index, 1, left2).wait_send()
    for t in range(4):
        back, ahead = wrap(q - t), wrap(q + t)
        remainder(back, 0, right2).wait_send()
        if t > 0:
            message(back, 0, 0, right2).wait_send()
            message(ahead, 1, 1, left2).wait_send()
        if t < 3:
            remainder(ahead, 1, left2).wait_send()
        if 0 < t < 3:
            message(back, 1, 0, right2).wait_send()
            message(ahead, 0, 1, left2).wait_send()

    states(core, x, 0, partner).wait_send()
    states(core, x, 1, partner).wait_send()
    states(core, x - way, 2, partner).wait_send()
    for d in range(TENSORS):
        states(core, x + d, 3, partner).wait_send()
    codes.wait_send()
    for n, peer in enumerate(peers):
        result(n, peer).wait_send()
    for d in range(1, RING):
        along_line(d, wrap(z + d), z).wait_send()
    own_plane.wait()
    for d in range(1, 2 * RING):
        across_plane(d, turn(d), here).wait_send()
        across_plane(d, turn(d), turn(d)).wait_recv()
    out_ref[...] = plane_in[...]


def head(main, rest, hid, code, gain, place, live):
    rows, feats, slots = hid.shape[1], hid.shape[0], RING * RING
    depth = TENSORS * feats
    any_space = pl.BlockSpec(memory_space=pl.ANY)
    vmem = pl.BlockSpec(memory_space=pltpu.VMEM)
    dma = pltpu.SemaphoreType.DMA
    return pl.pallas_call(
        head_kernel,
        out_shape=jax.ShapeDtypeStruct((2 * RING, RING, 128), F32),
        in_specs=[any_space] * 4 + [vmem] * 3,
        out_specs=vmem,
        scratch_shapes=[
            pltpu.VMEM((slots, MAIN, depth), jnp.bfloat16),
            pltpu.VMEM((slots, 16, 128), jnp.bfloat16),
            pltpu.VMEM((2, TENSORS, feats, rows), jnp.bfloat16),
            pltpu.VMEM((2, 1, rows), jnp.int32),
            pltpu.VMEM((depth, 2 * rows), jnp.bfloat16),
            pltpu.VMEM((slots * 16, 128), F32),
            pltpu.VMEM((slots * 2, depth), jnp.bfloat16),
            pltpu.VMEM((4, 8, 2 * rows), F32),
            pltpu.VMEM((2, 8, rows), F32),
            pltpu.VMEM((2 * TENSORS, 8, rows), F32),
            pltpu.VMEM((rows, RING * 128), jnp.bfloat16),
            pltpu.VMEM((2, rows), F32),
            pltpu.VMEM((RING, 8, 128), F32),
            pltpu.VMEM((RING, 8, 128), F32),
            pltpu.VMEM((2 * RING, RING, 128), F32),
            pltpu.VMEM((2 * RING, RING, 128), F32),
            dma((2, RING)), dma((2, 2, RING)), dma((RING, 2)), dma((2, RING, 2)), dma((2, RING)), dma((2, RING)),
            dma((RING,)), dma((2, RING)),
            dma((2, TENSORS)), dma((4, TENSORS)),
            dma((2,)), dma((2 * TENSORS,)), dma((2 * TENSORS,)), dma((4,)),
            dma((RING,)), dma((RING,)), dma((2 * RING,)), dma((2 * RING,)),
        ],
        compiler_params=pltpu.CompilerParams(
            collective_id=0, has_side_effects=True, vmem_limit_bytes=48 << 20),
    )(main, rest, hid, code, gain, place, live)


def body(hidden, gain, head_weight, targets, row_count, dest):
    rows = hidden.shape[0]
    cols = head_weight.shape[1]
    groups = 2 * RING * RING
    turned = head_weight.T
    rest = turned[MAIN:].reshape(16, 128)
    owner, column = targets // (cols * groups), targets % cols
    device = (targets // cols) % groups
    near, zy = device % 2, device // 2
    zi, yi = zy // RING, zy % RING
    z, y = lax.axis_index("z"), lax.axis_index("y")
    gone = (jnp.where(near == 0, zi - z, yi - y) + RING) % RING
    order = jnp.where(gone < RING // 2, 2 * gone, 2 * (RING - gone) - 1)
    slot = jnp.where(near == 0, yi, zi) * RING + order
    index = jnp.where(column < MAIN, slot * MAIN + column, RING * RING * MAIN + slot * 2 + column - MAIN)
    code = ((owner * 2 + near) * 4096 + index).reshape(1, rows)
    share = rows // groups
    rank = (dest // rows) * share + dest % share
    line = rows // RING
    place = (rank // line) * 128 + rank % line
    live = (jnp.arange(rows, dtype=jnp.int32) < row_count[0]).astype(jnp.int32)
    got = head(turned, rest, hidden.T, code, gain.reshape(-1, 1), place.reshape(-1, 1), live.reshape(1, -1))
    got = jnp.moveaxis(got[:, :, :2 * share], 1, 0)
    return got[:, :, :share].reshape(rows), got[:, :, share:].reshape(rows)


def solution(mesh):
    tensor = mesh.devices.shape[1]
    fine = Mesh(mesh.devices.reshape(RING, RING, 2, tensor), ("z", "y", "core", "tensor"))
    group = ("z", "y", "core")
    in_specs = (P(group, "tensor"), P(), P(None, ("tensor", "z", "y", "core")), P(group), P(group), P(group))
    return jax.shard_map(body, mesh=fine, in_specs=in_specs, out_specs=(P(group), P(group)), check_vma=False)
```

```python
import functools

import jax
import jax.numpy as jnp
from jax import lax
from jax.experimental import pallas as pl
from jax.experimental.pallas import tpu as pltpu
from jax.sharding import Mesh, PartitionSpec as P

RING = 8
TENSORS = 4
MAIN = 48
CHUNK = 256
F32 = jnp.float32


def zigzag(i):
    return ((i + 1) >> 1) * (1 - 2 * (i & 1))


def head_kernel(main_hbm, rest_hbm, hid_hbm, gain_row, notes, out_ref,
                wbuf, lbuf, hbuf, cbuf, normed, wide_rest, rest, stats, packed, gath,
                gain_ref, select, values, line_out, line_in, plane_out, plane_in,
                b_recv, b_send, m_recv, m_send, o_recv, o_send, r_recv, r_send, h_recv, h_send, c_sem, s_recv, s_send, local_sem,
                l_recv, l_send, p_recv, p_send):
    z, y = lax.axis_index("z"), lax.axis_index("y")
    core, x = lax.axis_index("core"), lax.axis_index("tensor")
    rows = hid_hbm.shape[1]
    feats = hid_hbm.shape[0]
    p = z + core * (y - z)
    q = y + core * (z - y)

    def wrap(v):
        return (v + 2 * RING) & (RING - 1)

    def at(pp, qq):
        return (pp + core * (qq - pp), qq + core * (pp - qq), core, x)

    def at_x(xx, cc):
        return (z, y, cc, (xx + 2 * TENSORS) & (TENSORS - 1))

    right1, left1 = at(wrap(p + 1), q), at(wrap(p - 1), q)
    right2, left2 = at(p, wrap(q + 1)), at(p, wrap(q - 1))
    partner = at_x(x, 1 - core)
    slot0 = q * RING

    locals_ = [
        pltpu.make_async_copy(main_hbm.at[pl.ds(0, MAIN)], wbuf.at[slot0], local_sem.at[0]),
        pltpu.make_async_copy(rest_hbm, lbuf.at[slot0], local_sem.at[1]),
        pltpu.make_async_copy(hid_hbm, hbuf.at[core, x], local_sem.at[2]),
    ]
    for copy in locals_:
        copy.start()
    cbuf[core] = notes[pl.ds(0, 1), :]
    gain_ref[...] = jnp.broadcast_to(gain_row[...], (128, gain_row.shape[1])).T
    barrier = pltpu.get_barrier_semaphore()
    peers = [at_x(x + d, c) for d in range(TENSORS) for c in (core, 1 - core)][1:]
    for peer in [right1, left1, right2, left2] + peers:
        pl.semaphore_signal(barrier, inc=1, device_id=peer, device_id_type=pl.DeviceIdType.MESH)
    for copy in locals_:
        copy.wait()
    pl.semaphore_wait(barrier, 4 + len(peers))

    def block(index, landing, kind, target):
        return [
            pltpu.make_async_remote_copy(
                src_ref=buf.at[slot0 + index], dst_ref=buf.at[slot0 + landing],
                send_sem=b_send.at[kind, n, index], recv_sem=b_recv.at[n, landing],
                device_id=target, device_id_type=pl.DeviceIdType.MESH)
            for n, buf in enumerate((wbuf, lbuf))
        ]

    def message(group, half, kind, target):
        part = wbuf.at[pl.ds(group * RING + half * 4, 4)]
        return pltpu.make_async_remote_copy(
            src_ref=part, dst_ref=part,
            send_sem=m_send.at[kind, group, half], recv_sem=m_recv.at[group, half],
            device_id=target, device_id_type=pl.DeviceIdType.MESH)

    def single(group, index, kind, target):
        part = wbuf.at[group * RING + index]
        return pltpu.make_async_remote_copy(
            src_ref=part, dst_ref=part,
            send_sem=o_send.at[kind, index], recv_sem=o_recv.at[kind, index],
            device_id=target, device_id_type=pl.DeviceIdType.MESH)

    def remainder(group, kind, target):
        part = lbuf.at[pl.ds(group * RING, RING)]
        return pltpu.make_async_remote_copy(
            src_ref=part, dst_ref=part,
            send_sem=r_send.at[kind, group], recv_sem=r_recv.at[group],
            device_id=target, device_id_type=pl.DeviceIdType.MESH)

    def states(cc, xx, kind, target):
        xs = (xx + 2 * TENSORS) & (TENSORS - 1)
        return pltpu.make_async_remote_copy(
            src_ref=hbuf.at[cc, xs], dst_ref=hbuf.at[cc, xs],
            send_sem=h_send.at[kind, xs], recv_sem=h_recv.at[cc, xs],
            device_id=target, device_id_type=pl.DeviceIdType.MESH)

    codes = pltpu.make_async_remote_copy(
        src_ref=cbuf.at[core], dst_ref=cbuf.at[core], send_sem=c_sem.at[0], recv_sem=c_sem.at[1],
        device_id=partner, device_id_type=pl.DeviceIdType.MESH)
    way = 1 - 2 * core
    for copy in block(0, 1, 0, right1) + block(0, 2, 1, left1):
        copy.start()
    single(q, 0, 0, right2).start()
    single(q, 0, 1, left2).start()
    states(core, x, 0, at_x(x + 1, core)).start()
    states(core, x, 1, at_x(x - 1, core)).start()
    states(core, x, 3, partner).start()
    codes.start()

    def first(i):
        for copy in block(i, i, 0, right1):
            copy.wait_recv()
        onward = []
        if i in (1, 3, 5):
            onward = block(i, i + 2, 0, right1)
        if i in (2, 4):
            onward = block(i, i + 2, 1, left1)
        for copy in onward:
            copy.start()
        single(q, i, 0, right2).start()
        single(q, i, 1, left2).start()

    for i in range(1, 4):
        first(i)
    for d in (-1, 1):
        states(core, x + d, 0, partner).wait_recv()
    states(core, x - way, 2, at_x(x + way, core)).start()
    for d in (-1, 1):
        states(core, x + d, 3, partner).start()
    for i in range(4, 8):
        first(i)

    remainder(q, 0, right2).start()
    remainder(q, 1, left2).start()

    def second(t, half):
        back, ahead = wrap(q - t), wrap(q + t)
        if half == 1:
            remainder(back, 0, right2).wait_recv()
            if t < 4:
                remainder(back, 0, right2).start()
                remainder(ahead, 1, left2).wait_recv()
            if t < 3:
                remainder(ahead, 1, left2).start()
        if t == 1:
            for index in range(4 * half, 4 * half + 4):
                single(back, index, 0, right2).wait_recv()
        elif t < 4 or half == 0:
            message(back, half, 0, right2).wait_recv()
        if t < 3 or (t == 3 and half == 0):
            message(back, half, 0, right2).start()
        if t == 1:
            for index in range(4 * half, 4 * half + 4):
                single(ahead, index, 1, left2).wait_recv()
        elif t < 4 or half == 1:
            message(ahead, half, 1, left2).wait_recv()
        if t < 3 or (t == 3 and half == 1):
            message(ahead, half, 1, left2).start()

    states(core, x + 2, 0, partner).wait_recv()
    states(core, x + 2, 3, partner).start()
    second(1, 0)
    spots = lax.broadcasted_iota(jnp.int32, select.shape, 1)
    places = jnp.broadcast_to(notes[pl.ds(1, 1), :].astype(F32), (128, rows)).T
    select[...] = jnp.where(spots == places[:, :1].astype(jnp.int32), 1.0, 0.0).astype(jnp.bfloat16)
    line_out[...] = jnp.zeros(line_out.shape, F32)
    second(1, 1)

    for d in range(TENSORS):
        states(1 - core, x + d, 0, partner).wait_recv()
    codes.wait_recv()
    for c in range(2):
        power = jnp.zeros((1, rows), F32)
        for d in range(TENSORS):
            part = hbuf[c, d].astype(F32)
            power += jnp.sum(part * part, axis=0, keepdims=True)
        scale = lax.rsqrt(power / (TENSORS * feats) + 1e-06)
        for d in range(TENSORS):
            span = pl.ds(d * feats, feats)
            part = hbuf[c, d].astype(F32) * scale * gain_ref[span, :1]
            normed[span, pl.ds(c * rows, rows)] = part.astype(jnp.bfloat16)
    stats[0] = jnp.full(stats.shape[1:], -1e30, F32)
    for n in range(1, 4):
        stats[n] = jnp.zeros(stats.shape[1:], F32)
    mine = (x * 2 + core) * 4096
    per = rows // CHUNK

    def update(weights, count, base, r):
        cols = pl.ds(pl.multiple_of(r * CHUNK, CHUNK), CHUNK)
        logits = jnp.dot(weights, normed[:, cols], preferred_element_type=F32)
        cube = logits.reshape(count // 8, 8, CHUNK)
        half = r // per
        span = pl.ds(pl.multiple_of((r - half * per) * CHUNK, CHUNK), CHUNK)
        wanted = cbuf[half, :, span] - (mine + base)
        ids = lax.broadcasted_iota(jnp.int32, (count, CHUNK), 0)
        old = stats[0, :, cols]
        top = jnp.maximum(old, jnp.max(cube, axis=0))
        factor = jnp.exp(old - top)
        weight = jnp.exp(cube - top[None])
        stats[0, :, cols] = top
        stats[1, :, cols] = stats[1, :, cols] * factor + jnp.sum(weight, axis=0)
        stats[2, :, cols] = stats[2, :, cols] * factor + jnp.sum(weight * cube, axis=0)
        hit = jnp.where(ids == wanted, logits, 0.0).reshape(count // 8, 8, CHUNK)
        stats[3, :, cols] = stats[3, :, cols] + jnp.sum(hit, axis=0)

    chunks = 2 * per

    def unit(u):
        k = u // chunks
        r = u - k * chunks
        g = wrap(q + zigzag(k))
        weights = wbuf[pl.ds(pl.multiple_of(g * RING, RING), RING)].reshape(RING * MAIN, -1)
        update(weights, RING * MAIN, g * (RING * MAIN), r)

    def units(low, high):
        @pl.loop(low, high)
        def _(u):
            unit(u)

    second(2, 0)
    units(0, 4)
    units(4, 8)
    second(2, 1)
    units(8, 12)
    second(3, 0)
    units(12, 16)
    second(3, 1)
    units(16, 28)
    second(4, 0)
    second(4, 1)
    units(28, 32)

    total = RING * RING * 2
    wide_rest[...] = lbuf[...].astype(F32).reshape(total * 8, 128)
    for k in range(8):
        rest[:, pl.ds(k * 128, 128)] = wide_rest[pl.ds(k, total, stride=8), :].astype(jnp.bfloat16)

    @pl.loop(0, chunks)
    def _(r):
        update(rest[...], total, RING * RING * MAIN, r)

    top = jnp.max(stats[0], axis=0, keepdims=True)
    factor = jnp.exp(stats[0] - top)
    lines = [top] + [jnp.sum(stats[n] * factor, axis=0, keepdims=True) for n in (1, 2)]
    lines.append(jnp.sum(stats[3], axis=0, keepdims=True))
    for c in range(2):
        for n, line in enumerate(lines):
            packed[c, pl.ds(n, 1), :] = line[:, c * rows:(c + 1) * rows]
        packed[c, pl.ds(4, 4), :] = jnp.zeros((4, rows), F32)
    who = x * 2 + core

    def result(n, peer):
        return pltpu.make_async_remote_copy(
            src_ref=packed.at[peer[2]], dst_ref=gath.at[who],
            send_sem=s_send.at[n], recv_sem=s_recv.at[who],
            device_id=peer, device_id_type=pl.DeviceIdType.MESH)

    def result_from(n, peer):
        source = peer[3] * 2 + peer[2]
        return pltpu.make_async_remote_copy(
            src_ref=packed.at[core], dst_ref=gath.at[source],
            send_sem=s_send.at[n], recv_sem=s_recv.at[source],
            device_id=peer, device_id_type=pl.DeviceIdType.MESH)

    for n, peer in enumerate(peers):
        result(n, peer).start()
    own = pltpu.make_async_copy(packed.at[core], gath.at[who], local_sem.at[0])
    own.start()

    own.wait()
    for n, peer in enumerate(peers):
        result_from(n, peer).wait_recv()

    tops = gath[:, 0, :]
    top = jnp.max(tops, axis=0, keepdims=True)
    factor = jnp.exp(tops - top)
    mass = jnp.sum(gath[:, 1, :] * factor, axis=0, keepdims=True)
    moment = jnp.sum(gath[:, 2, :] * factor, axis=0, keepdims=True)
    picked = jnp.sum(gath[:, 3, :], axis=0, keepdims=True)
    live = notes[pl.ds(2, 1), :] > 0
    lse = top + jnp.log(mass)
    values[pl.ds(0, 1), :] = jnp.where(live, picked - lse, 0.0)
    values[pl.ds(1, 1), :] = jnp.where(live, lse - moment / mass, 0.0)
    exact = values[...]
    high = exact.astype(jnp.bfloat16)
    left = exact - high.astype(F32)
    middle = left.astype(jnp.bfloat16)
    low = (left - middle.astype(F32)).astype(jnp.bfloat16)
    ordered = jnp.zeros((2, select.shape[1]), F32)
    for term in (low, middle, high):
        ordered += jnp.dot(term, select[...], preferred_element_type=F32)
    for n in range(RING):
        line_out[n, pl.ds(0, 2), :] = ordered[:, n * 128:(n + 1) * 128]

    def along_line(d, other, source):
        return pltpu.make_async_remote_copy(
            src_ref=line_out.at[other], dst_ref=line_in.at[source],
            send_sem=l_send.at[d], recv_sem=l_recv.at[source],
            device_id=(other, y, core, x), device_id_type=pl.DeviceIdType.MESH)

    own_line = pltpu.make_async_copy(line_out.at[z], line_in.at[z], local_sem.at[1])
    for d in range(1, RING):
        along_line(d, wrap(z + d), z).start()
    own_line.start()
    own_line.wait()
    for d in range(1, RING):
        along_line(d, wrap(z + d), wrap(z + d)).wait_recv()
    first_half, second_half = line_in[:, 0, :], line_in[:, 1, :]
    lanes = lax.broadcasted_iota(jnp.int32, (RING, 128), 1)
    for n in range(2 * RING):
        plane_out[n] = jnp.where(
            lanes < 4, pltpu.roll(first_half, (128 - 4 * n) % 128, 1),
            pltpu.roll(second_half, (132 - 4 * n) % 128, 1))
    here = y * 2 + core

    def across_plane(d, other, source):
        return pltpu.make_async_remote_copy(
            src_ref=plane_out.at[other], dst_ref=plane_in.at[source],
            send_sem=p_send.at[d], recv_sem=p_recv.at[source],
            device_id=(z, other >> 1, other & 1, x), device_id_type=pl.DeviceIdType.MESH)

    def turn(d):
        return (here + d) & (2 * RING - 1)

    own_plane = pltpu.make_async_copy(plane_out.at[here], plane_in.at[here], local_sem.at[2])
    for d in range(1, 2 * RING):
        across_plane(d, turn(d), here).start()
    own_plane.start()

    for i in (0, 1, 3, 5):
        for copy in block(i, i, 0, right1):
            copy.wait_send()
    for i in (0, 2, 4):
        for copy in block(i, i, 1, left1):
            copy.wait_send()
    for index in range(RING):
        single(q, index, 0, right2).wait_send()
        single(q, index, 1, left2).wait_send()
    for t in range(4):
        back, ahead = wrap(q - t), wrap(q + t)
        remainder(back, 0, right2).wait_send()
        if t > 0:
            message(back, 0, 0, right2).wait_send()
            message(ahead, 1, 1, left2).wait_send()
        if t < 3:
            remainder(ahead, 1, left2).wait_send()
        if 0 < t < 3:
            message(back, 1, 0, right2).wait_send()
            message(ahead, 0, 1, left2).wait_send()

    states(core, x, 0, partner).wait_send()
    states(core, x, 1, partner).wait_send()
    states(core, x - way, 2, partner).wait_send()
    for d in range(TENSORS):
        states(core, x + d, 3, partner).wait_send()
    codes.wait_send()
    for n, peer in enumerate(peers):
        result(n, peer).wait_send()
    for d in range(1, RING):
        along_line(d, wrap(z + d), z).wait_send()
    own_plane.wait()
    for d in range(1, 2 * RING):
        across_plane(d, turn(d), here).wait_send()
        across_plane(d, turn(d), turn(d)).wait_recv()
    out_ref[...] = plane_in[...]


def head(main, rest, hid, gain, notes):
    rows, feats, slots = hid.shape[1], hid.shape[0], RING * RING
    depth = TENSORS * feats
    any_space = pl.BlockSpec(memory_space=pl.ANY)
    vmem = pl.BlockSpec(memory_space=pltpu.VMEM)
    dma = pltpu.SemaphoreType.DMA
    return pl.pallas_call(
        head_kernel,
        out_shape=jax.ShapeDtypeStruct((2 * RING, RING, 128), F32),
        in_specs=[any_space] * 3 + [vmem] * 2,
        out_specs=vmem,
        scratch_shapes=[
            pltpu.VMEM((slots, MAIN, depth), jnp.bfloat16),
            pltpu.VMEM((slots, 16, 128), jnp.bfloat16),
            pltpu.VMEM((2, TENSORS, feats, rows), jnp.bfloat16),
            pltpu.VMEM((2, 1, rows), jnp.int32),
            pltpu.VMEM((depth, 2 * rows), jnp.bfloat16),
            pltpu.VMEM((slots * 16, 128), F32),
            pltpu.VMEM((slots * 2, depth), jnp.bfloat16),
            pltpu.VMEM((4, 8, 2 * rows), F32),
            pltpu.VMEM((2, 8, rows), F32),
            pltpu.VMEM((2 * TENSORS, 8, rows), F32),
            pltpu.VMEM((depth, 128), F32),
            pltpu.VMEM((rows, RING * 128), jnp.bfloat16),
            pltpu.VMEM((2, rows), F32),
            pltpu.VMEM((RING, 8, 128), F32),
            pltpu.VMEM((RING, 8, 128), F32),
            pltpu.VMEM((2 * RING, RING, 128), F32),
            pltpu.VMEM((2 * RING, RING, 128), F32),
            dma((2, RING)), dma((2, 2, RING)), dma((RING, 2)), dma((2, RING, 2)), dma((2, RING)), dma((2, RING)),
            dma((RING,)), dma((2, RING)),
            dma((2, TENSORS)), dma((4, TENSORS)),
            dma((2,)), dma((2 * TENSORS,)), dma((2 * TENSORS,)), dma((4,)),
            dma((RING,)), dma((RING,)), dma((2 * RING,)), dma((2 * RING,)),
        ],
        compiler_params=pltpu.CompilerParams(
            collective_id=0, has_side_effects=True, vmem_limit_bytes=48 << 20),
    )(main, rest, hid, gain, notes)


def body(hidden, gain, head_weight, targets, row_count, dest):
    rows = hidden.shape[0]
    cols = head_weight.shape[1]
    groups = 2 * RING * RING
    turned = head_weight.T
    rest = turned[MAIN:].reshape(16, 128)
    owner, column = targets // (cols * groups), targets % cols
    device = (targets // cols) % groups
    near, zy = device % 2, device // 2
    zi, yi = zy // RING, zy % RING
    z, y = lax.axis_index("z"), lax.axis_index("y")
    gone = (jnp.where(near == 0, zi - z, yi - y) + RING) % RING
    order = jnp.where(gone < RING // 2, 2 * gone, 2 * (RING - gone) - 1)
    slot = jnp.where(near == 0, yi, zi) * RING + order
    index = jnp.where(column < MAIN, slot * MAIN + column, RING * RING * MAIN + slot * 2 + column - MAIN)
    code = ((owner * 2 + near) * 4096 + index)
    share = rows // groups
    rank = (dest // rows) * share + dest % share
    line = rows // RING
    place = (rank // line) * 128 + rank % line
    live = (jnp.arange(rows, dtype=jnp.int32) < row_count[0]).astype(jnp.int32)
    notes = jnp.stack([code, place, live])
    got = head(turned, rest, hidden.T, gain.reshape(1, -1), notes)
    got = jnp.moveaxis(got[:, :, :2 * share], 1, 0)
    return got[:, :, :share].reshape(rows), got[:, :, share:].reshape(rows)


def solution(mesh):
    tensor = mesh.devices.shape[1]
    fine = Mesh(mesh.devices.reshape(RING, RING, 2, tensor), ("z", "y", "core", "tensor"))
    group = ("z", "y", "core")
    in_specs = (P(group, "tensor"), P(), P(None, ("tensor", "z", "y", "core")), P(group), P(group), P(group))
    return jax.shard_map(body, mesh=fine, in_specs=in_specs, out_specs=(P(group), P(group)), check_vma=False)
```
